32 devices in a mesh: groups: 2 (over y), frame: 8 (over z, x), row: 2 (over core).
Axes of the slice: x: 2, y: 2, z: 4, core: 2. Of those that a mesh axis runs over, the one named last changes fastest.
Arguments:
- latents: bfloat16 [16, 1024, 256], P(('groups', 'frame'), 'row'), parts along dimension 0, may hold values from -8 to 8
- ref_frames: int32 [16, 2], P(('groups', 'frame')), parts along dimension 0, may hold values from 0 to 7, as said below
- windows: int32 [16], P(('groups', 'frame')), parts along dimension 0, may hold values from 1 to 2, as said below
- quant_level: int32 [16], P(('groups', 'frame')), parts along dimension 0, may hold values from 0 to 63
- quant_scale: float32 [64, 256], replicated, may hold values from 0.5 to 2
- shared_proj: bfloat16 [256, 256], replicated, may hold values from -0.375 to 0.375
- value_proj: bfloat16 [256, 256], replicated, may hold values from -0.375 to 0.375
- output_proj: bfloat16 [256, 256], replicated, may hold values from -0.75 to 0.75
- conv_taps: bfloat16 [3, 256, 256], replicated, may hold values from -0.21875 to 0.21875
- cotangent: bfloat16 [16, 1024, 256], P(('groups', 'frame'), 'row'), parts along dimension 0, may hold values from -6 to 6
Outputs:
- coded_latent: bfloat16 [16, 1024, 256], P(('groups', 'frame'), 'row'), parts along dimension 0
- grad_latents: bfloat16 [16, 1024, 256], P(('groups', 'frame'), 'row'), parts along dimension 0
- grad_shared: float32 [512, 256], P('groups'), parts along dimension 0
- grad_values: float32 [512, 256], P('groups'), parts along dimension 0
- grad_output: float32 [512, 256], P('groups'), parts along dimension 0
- grad_taps: float32 [6, 256, 256], P('groups'), parts along dimension 0
The draws below stay inside these ranges and needn't reach their ends.
There are 2 independent parts, one for each index of `groups`. The reference program is written for one: setup_inputs(seed, part) draws one part's arguments, and reference() takes and returns one part's arrays. A program takes and returns all parts, laid end to end along the dimension named above; an argument that names none is the same for every part. Nothing has to cross between parts.
Inputs may be any that keep to these rules, and one draw needn't show every extreme that they name: ref_frames[f, s] differs from f by a power of two no larger than 2 ** 2, and that largest distance occurs. `windows`: some frame has a window of 2 rows.
All inputs are finite; a program needn't handle non-finite values.
Results may differ from the reference program's by a relative error of at most 0.0045.
The reference program's roundings to bfloat16 on the way count: a program that leaves them out, or rounds other values in their place, can miss the bound.
Values may be sent and summed in bfloat16 or wider, within the bound.
A program may use at most 128 MiB of HBM per device.

```python
import math
import jax
import jax.numpy as jnp
from jax import lax

C = 256
HEADS = 8
DH = 32
COLS = 64
QROWS = 8
WMAX = 2
LEVELS = 3
NQ = 64
FRAMES = 8
HROWS = 16
TOKF = 1024


def draw_latents(key, part):
    shape = (FRAMES, HROWS * COLS, C)
    values = jnp.clip(jax.random.normal(jax.random.fold_in(key, 1), shape, jnp.float32), -4.0, 4.0)
    return values.astype(jnp.bfloat16)


def draw_ref_frames(key, part):
    depth = jax.random.randint(jax.random.fold_in(key, 1), (FRAMES, 2), 0, LEVELS)
    depth = depth.at[0, 0].set(LEVELS - 1)
    distance = jnp.left_shift(jnp.ones((FRAMES, 2), jnp.int32), depth.astype(jnp.int32))
    side = jax.random.randint(jax.random.fold_in(key, 2), (FRAMES, 2), 0, 2)
    frame_ids = jnp.arange(FRAMES, dtype=jnp.int32)[:, None]
    earlier = frame_ids - distance
    later = frame_ids + distance
    pick_earlier = jnp.where(side == 0, earlier >= 0, later > FRAMES - 1)
    return jnp.where(pick_earlier, earlier, later).astype(jnp.int32)


def draw_windows(key, part):
    window = jax.random.randint(jax.random.fold_in(key, 3), (FRAMES,), 1, WMAX + 1)
    return window.at[0].set(WMAX).astype(jnp.int32)


def with_ends(drawn, stream_key, low, largest):
    shape = drawn.shape
    place = [jax.random.randint(jax.random.fold_in(stream_key, axis), (), 0, shape[axis]) for axis in range(len(shape))]
    drawn = drawn.at[tuple(place)].set(low)
    longest = shape.index(max(shape))
    place[longest] = (place[longest] + 1) % shape[longest]
    return drawn.at[tuple(place)].set(largest)


def shard_levels(key, extent, shards, low, largest):
    factor_of, own = 1.0, jax.random.fold_in(key, 6)
    for position, parts in shards:
        draws = jnp.exp(jax.random.uniform(jax.random.fold_in(own, position), (parts,), jnp.float32, low / len(shards), largest / len(shards)))
        factor_of = factor_of * jnp.repeat(draws, extent[position] // parts).reshape([-1 if axis == position else 1 for axis in range(len(extent))])
    return factor_of


def noise(rng, dims, scale, most, split=(), kind=jnp.bfloat16):
    loudness = shard_levels(rng, dims, split, -0.22, 0.18) if split else 1.0
    array = jax.random.normal(rng, dims, jnp.float32) * scale * loudness
    return jnp.minimum(jnp.maximum(array, -most), most).astype(kind)


def setup_inputs(seed: int = 0, part: int = 0) -> dict:
    seeds = jax.random.split(jax.random.key(seed), 11)
    own_keys = jax.random.split(jax.random.fold_in(seeds[10], part), 11)
    latents = draw_latents(jax.random.fold_in(jax.random.fold_in(seeds[10], part), 71), part)
    ref_frames = draw_ref_frames(jax.random.fold_in(jax.random.fold_in(seeds[10], part), 71), part)
    windows = draw_windows(jax.random.fold_in(jax.random.fold_in(seeds[10], part), 71), part)
    quant_level = with_ends(jax.random.randint(own_keys[3], (FRAMES,), 0, NQ), jax.random.fold_in(own_keys[3], 1), 0, NQ - 1).astype(jnp.int32)
    quant_scale = jnp.clip(jnp.exp(jax.random.uniform(seeds[4], (NQ, C), jnp.float32, math.log(0.5), math.log(2.0))), 0.5, 2.0)
    shared_proj = noise(seeds[5], (C, C), C ** -0.5, 0.375)
    value_proj = noise(seeds[6], (C, C), C ** -0.5, 0.375)
    output_proj = noise(seeds[7], (C, C), (C // 4) ** -0.5, 0.75)
    conv_taps = noise(seeds[8], (3, C, C), (3 * C) ** -0.5, 0.21875)
    cotangent = noise(own_keys[9], (FRAMES, TOKF, C), 1.0, 6.0, ((0, 8), (1, 2)))
    return {"latents": latents, "ref_frames": ref_frames, "windows": windows, "quant_level": quant_level, "quant_scale": quant_scale, "shared_proj": shared_proj, "value_proj": value_proj, "output_proj": output_proj, "conv_taps": conv_taps, "cotangent": cotangent}


SCORE_GAIN = 1.5
LAST_DIMS = (((1,), (1,)), ((), ()))
FIRST_DIMS = (((0,), (0,)), ((), ()))

def split_heads(block):
    return jnp.transpose(block.reshape(block.shape[0], HEADS, DH), (1, 0, 2))

def merge_heads(block):
    return jnp.transpose(block, (1, 0, 2)).reshape(block.shape[1], HEADS * DH)

def head_weights(query_head, key_head, allowed):
    scores = jnp.dot(query_head, key_head.T, preferred_element_type=jnp.float32) * (SCORE_GAIN / math.sqrt(DH))
    scores = jnp.where(allowed, scores, -jnp.inf)
    row_max = lax.optimization_barrier(jnp.max(scores, axis=1, keepdims=True))
    exp_terms = jnp.where(allowed, jnp.exp(scores - row_max), 0.0)
    return exp_terms / lax.optimization_barrier(jnp.sum(exp_terms, axis=1, keepdims=True))

def block_forward(query, keys, values, allowed):

    def one_head(head_parts):
        query_head, key_head, value_head = head_parts
        weights = head_weights(query_head, key_head, allowed)
        return jnp.dot(weights.astype(jnp.bfloat16), value_head, preferred_element_type=jnp.float32)
    result = lax.map(one_head, (split_heads(query), split_heads(keys), split_heads(values)))
    return merge_heads(result).astype(jnp.bfloat16)

def block_backward(query, keys, values, allowed, upstream):

    def one_head(head_parts):
        query_head, key_head, value_head, grad_head = head_parts
        weights = head_weights(query_head, key_head, allowed)
        prob = weights.astype(jnp.bfloat16)
        grad_prob = jnp.dot(grad_head, value_head.T, preferred_element_type=jnp.float32)
        value_grad = jnp.dot(prob.T, grad_head, preferred_element_type=jnp.float32)
        row_inner = lax.optimization_barrier(jnp.sum(weights * grad_prob, axis=1, keepdims=True))
        grad_score = (weights * (grad_prob - row_inner) * (SCORE_GAIN / math.sqrt(DH))).astype(jnp.bfloat16)
        query_grad = jnp.dot(grad_score, key_head, preferred_element_type=jnp.float32)
        key_grad = jnp.dot(grad_score.T, query_head, preferred_element_type=jnp.float32)
        return (query_grad, key_grad, value_grad)
    query_grad, key_grad, value_grad = lax.map(one_head, (split_heads(query), split_heads(keys), split_heads(values), split_heads(upstream)))
    return (merge_heads(query_grad), merge_heads(key_grad), merge_heads(value_grad))

def allowed_mask(begin_row, window, total_rows):
    key_span = QROWS + 2 * WMAX
    query_rows = begin_row + jnp.repeat(jnp.arange(QROWS, dtype=jnp.int32), COLS)
    key_rows = jnp.tile(jnp.repeat(begin_row - WMAX + jnp.arange(key_span, dtype=jnp.int32), COLS), 2)
    nearby = jnp.abs(query_rows[:, None] - key_rows[None, :]) <= window
    inside = (key_rows >= 0) & (key_rows < total_rows)
    return nearby & inside[None, :]

def add_window(summed, addend, begin_row):
    current = lax.dynamic_slice_in_dim(summed, begin_row, addend.shape[1], 1)
    return lax.dynamic_update_slice_in_dim(summed, current + addend, begin_row, 1)

def against(left_side, weight):
    return lax.dot_general(left_side, weight, LAST_DIMS, preferred_element_type=jnp.float32)

def cross_rows(left_side, right_side):
    return lax.dot_general(left_side, right_side, FIRST_DIMS, preferred_element_type=jnp.float32)

def exact_against(left_side, weight):
    return lax.dot_general(left_side, weight.astype(jnp.float32), LAST_DIMS, precision=lax.Precision.HIGHEST, preferred_element_type=jnp.float32)

def exact_cross(left_side, right_side):
    return lax.dot_general(left_side.astype(jnp.float32), right_side, FIRST_DIMS, precision=lax.Precision.HIGHEST, preferred_element_type=jnp.float32)

def reference(latents, ref_frames, windows, quant_level, quant_scale, shared_proj, value_proj, output_proj, conv_taps, cotangent):
    frames = latents.shape[0]
    width = latents.shape[2]
    flat_rows = latents.reshape(-1, width)
    queries = jnp.dot(flat_rows, shared_proj, preferred_element_type=jnp.float32).astype(jnp.bfloat16)
    value_rows = jnp.dot(flat_rows, value_proj, preferred_element_type=jnp.float32).astype(jnp.bfloat16)
    query_grid = queries.reshape(frames, HROWS, COLS, width)
    value_grid = value_rows.reshape(frames, HROWS, COLS, width)
    margins = ((0, 0), (WMAX, WMAX), (0, 0), (0, 0))
    query_pad = jnp.pad(query_grid, margins)
    value_pad = jnp.pad(value_grid, margins)
    key_span = QROWS + 2 * WMAX
    ext_rows = HROWS + 2 * WMAX
    block_ids = jnp.arange(HROWS // QROWS, dtype=jnp.int32)

    def gather_slots(frame):
        ref_pair = ref_frames[frame]
        keys = jnp.stack([query_pad[ref_pair[0]], query_pad[ref_pair[1]]])
        values = jnp.stack([value_pad[ref_pair[0]], value_pad[ref_pair[1]]])
        return (keys, values)

    def block_parts(frame, keys, values, block):
        begin_row = block * QROWS
        query = lax.dynamic_slice_in_dim(query_grid[frame], begin_row, QROWS, 0).reshape(-1, width)
        key_block = lax.dynamic_slice_in_dim(keys, begin_row, key_span, 1).reshape(-1, width)
        value_block = lax.dynamic_slice_in_dim(values, begin_row, key_span, 1).reshape(-1, width)
        allowed = allowed_mask(begin_row, windows[frame], HROWS)
        return (query, key_block, value_block, allowed)

    def frame_forward(frame):
        keys, values = gather_slots(frame)

        def one_block(block):
            query, key_block, value_block, allowed = block_parts(frame, keys, values, block)
            return block_forward(query, key_block, value_block, allowed)
        return lax.map(one_block, block_ids).reshape(HROWS * COLS, width)
    mixed_rows = lax.map(frame_forward, jnp.arange(frames, dtype=jnp.int32)).reshape(-1, width)
    residual = flat_rows.astype(jnp.float32) + jnp.dot(mixed_rows, output_proj, preferred_element_type=jnp.float32)
    hidden = residual.astype(jnp.bfloat16).reshape(frames, HROWS, COLS, width)
    hidden_pad = jnp.pad(hidden, ((0, 0), (1, 1), (0, 0), (0, 0)))
    context = jnp.zeros_like(residual)
    for tap_shift in (-1, 0, 1):
        shifted = hidden_pad[:, 1 + tap_shift:1 + tap_shift + HROWS].reshape(-1, width)
        context = context + jnp.dot(shifted, conv_taps[tap_shift + 1], preferred_element_type=jnp.float32)
    gain_rows = quant_scale[quant_level]
    coded_latent = ((residual + context).reshape(frames, -1, width) * gain_rows[:, None, :]).astype(jnp.bfloat16)
    grad_z = cotangent.astype(jnp.float32) * gain_rows[:, None, :]
    grad_zb = grad_z.astype(jnp.bfloat16)
    grad_pad = jnp.pad(grad_zb.reshape(frames, HROWS, COLS, width), ((0, 0), (1, 1), (0, 0), (0, 0)))
    grad_resid = grad_z.reshape(-1, width)
    for tap_shift in (-1, 0, 1):
        shifted = grad_pad[:, 1 - tap_shift:1 - tap_shift + HROWS].reshape(-1, width)
        grad_resid = grad_resid + against(shifted, conv_taps[tap_shift + 1])
    grad_rb = grad_resid.astype(jnp.bfloat16)
    grad_mixed = against(grad_rb, output_proj).astype(jnp.bfloat16).reshape(frames, HROWS, COLS, width)
    zero_sums = jnp.zeros((frames, ext_rows, COLS, width), jnp.float32)

    def frame_backward(running, frame):
        key_sums, value_sums = running
        keys, values = gather_slots(frame)

        def one_block(inner_sums, block):
            query_grad, key_grad, value_grad = inner_sums
            query, key_block, value_block, allowed = block_parts(frame, keys, values, block)
            begin_row = block * QROWS
            upstream = lax.dynamic_slice_in_dim(grad_mixed[frame], begin_row, QROWS, 0).reshape(-1, width)
            block_query, block_key, block_value = block_backward(query, key_block, value_block, allowed, upstream)
            query_grad = lax.dynamic_update_slice_in_dim(query_grad, block_query.reshape(QROWS, COLS, width), begin_row, 0)
            key_grad = add_window(key_grad, block_key.reshape(2, key_span, COLS, width), begin_row)
            value_grad = add_window(value_grad, block_value.reshape(2, key_span, COLS, width), begin_row)
            return ((query_grad, key_grad, value_grad), None)
        initial = (jnp.zeros((HROWS, COLS, width), jnp.float32), jnp.zeros((2, ext_rows, COLS, width), jnp.float32), jnp.zeros((2, ext_rows, COLS, width), jnp.float32))
        (query_grad, key_grad, value_grad), _ = lax.scan(one_block, initial, block_ids)
        ref_pair = ref_frames[frame]
        key_sums = key_sums.at[ref_pair[0]].add(key_grad[0]).at[ref_pair[1]].add(key_grad[1])
        value_sums = value_sums.at[ref_pair[0]].add(value_grad[0]).at[ref_pair[1]].add(value_grad[1])
        return ((key_sums, value_sums), query_grad)
    (key_sums, value_sums), query_grads = lax.scan(frame_backward, (zero_sums, zero_sums), jnp.arange(frames, dtype=jnp.int32))
    grad_proj = (query_grads + key_sums[:, WMAX:WMAX + HROWS]).reshape(-1, width)
    grad_vals = value_sums[:, WMAX:WMAX + HROWS].reshape(-1, width)
    grad_latents = grad_resid + exact_against(grad_proj, shared_proj) + exact_against(grad_vals, value_proj)
    grad_latents = grad_latents.astype(jnp.bfloat16).reshape(frames, -1, width)
    norm_scale = 1.0 / math.sqrt(frames * HROWS * COLS)
    grad_shared = exact_cross(flat_rows, grad_proj) * norm_scale
    grad_values = exact_cross(flat_rows, grad_vals) * norm_scale
    grad_output = cross_rows(mixed_rows, grad_rb) * norm_scale
    flat_grad = grad_zb.reshape(-1, width)
    grad_taps = jnp.stack([cross_rows(hidden_pad[:, 1 + tap_shift:1 + tap_shift + HROWS].reshape(-1, width), flat_grad) for tap_shift in (-1, 0, 1)]) * norm_scale
    return (coded_latent, grad_latents, grad_shared, grad_values, grad_output, grad_taps)
```

```python
import functools
import math

import jax
import jax.numpy as jnp
from jax import lax
from jax.experimental import pallas as pl
from jax.experimental.pallas import tpu as pltpu
from jax.sharding import PartitionSpec as P

HEADS = 8
DH = 32
COLS = 64
QBLK = 4
WMAX = 2
LEVELS = 3

SCORE_SCALE = 1.5 / math.sqrt(DH)
LOG2E = math.log2(math.e)
BF = jnp.bfloat16
F32 = jnp.float32


def mm(a, b, ca=1, cb=0):
    return lax.dot_general(a, b, (((ca,), (cb,)), ((), ())), preferred_element_type=F32)


def attention_kernel(
    bias_ref, q_ref, qt_ref, do_ref, dot_ref, k_ref, v_ref, kt_ref, vt_ref,
    mixt_ref, dqt_ref, dk_ref, dv_ref,
    s_scr, dp_scr, p_scr, ds_scr, qm_scr, dom_scr,
):
    tokens, width = q_ref.shape
    nq = QBLK * COLS
    span = (QBLK + 2 * WMAX) * COLS
    rows = span // COLS
    blocks = tokens // nq
    half = width // 2
    per_half = HEADS // 2
    lane = lax.broadcasted_iota(jnp.int32, (1, width), 1) // DH
    sub = lax.broadcasted_iota(jnp.int32, (half, 1), 0) // DH

    dk_ref[...] = jnp.zeros_like(dk_ref)
    dv_ref[...] = jnp.zeros_like(dv_ref)

    for b in range(blocks):
        q0 = b * nq
        qb = q_ref[q0 : q0 + nq, :]
        dob = do_ref[q0 : q0 + nq, :]
        for h in range(HEADS):
            keep = lane == h
            qm_scr[h * nq : (h + 1) * nq, :] = jnp.where(keep, qb, jnp.zeros_like(qb))
            dom_scr[h * nq : (h + 1) * nq, :] = jnp.where(keep, dob, jnp.zeros_like(dob))

        for hf in range(2):
            f0 = hf * half
            qth = qt_ref[f0 : f0 + half, q0 : q0 + nq]
            doth = dot_ref[f0 : f0 + half, q0 : q0 + nq]

            def one_head(hh, carry, hf=hf, f0=f0, qth=qth, doth=doth, q0=q0, b=b):
                keep = sub == hh
                qtm = jnp.where(keep, qth, jnp.zeros_like(qth))
                dotm = jnp.where(keep, doth, jnp.zeros_like(doth))
                for s in range(2):
                    s_scr[s * span : (s + 1) * span, :] = mm(
                        k_ref[s, q0 : q0 + span, f0 : f0 + half], qtm
                    )
                    dp_scr[s * span : (s + 1) * span, :] = mm(
                        v_ref[s, q0 : q0 + span, f0 : f0 + half], dotm
                    )
                m8 = jnp.full((8, nq), -jnp.inf, F32)
                for c in range(2 * rows):
                    x = s_scr[c * COLS : (c + 1) * COLS, :].reshape(COLS // 8, 8, nq)
                    m8 = jnp.maximum(m8, jnp.max(x, axis=0) + bias_ref[b, c % rows, :][None, :])
                m = jnp.max(m8, axis=0, keepdims=True)
                kk = SCORE_SCALE * LOG2E
                l8 = jnp.zeros((8, nq), F32)
                u8 = jnp.zeros((8, nq), F32)
                for c in range(2 * rows):
                    sl = slice(c * COLS, (c + 1) * COLS)
                    off = (bias_ref[b, c % rows, :][None, :] - m) * kk
                    p = jnp.exp2(s_scr[sl, :] * kk + off)
                    s_scr[sl, :] = p
                    l8 = l8 + jnp.sum(p.reshape(COLS // 8, 8, nq), axis=0)
                    u8 = u8 + jnp.sum((p * dp_scr[sl, :]).reshape(COLS // 8, 8, nq), axis=0)
                inv = 1.0 / jnp.sum(l8, axis=0, keepdims=True)
                ci = inv * SCORE_SCALE
                inner = jnp.sum(u8, axis=0, keepdims=True) * inv * ci
                col = pl.multiple_of((hf * per_half + hh) * nq, nq)
                for c in range(2 * rows):
                    sl = slice(c * COLS, (c + 1) * COLS)
                    p = s_scr[sl, :]
                    p_scr[sl, pl.ds(col, nq)] = (p * inv).astype(BF)
                    ds_scr[sl, pl.ds(col, nq)] = (p * (dp_scr[sl, :] * ci - inner)).astype(BF)
                r0 = pl.multiple_of(f0 + hh * DH, DH)
                mix = jnp.zeros((DH, nq), F32)
                dq = jnp.zeros((DH, nq), F32)
                for s in range(2):
                    ks = slice(s * span, (s + 1) * span)
                    mix = mix + mm(
                        vt_ref[s, pl.ds(r0, DH), q0 : q0 + span], p_scr[ks, pl.ds(col, nq)]
                    )
                    dq = dq + mm(
                        kt_ref[s, pl.ds(r0, DH), q0 : q0 + span], ds_scr[ks, pl.ds(col, nq)]
                    )
                mixt_ref[pl.ds(r0, DH), q0 : q0 + nq] = mix.astype(BF)
                dqt_ref[pl.ds(r0, DH), q0 : q0 + nq] = dq
                return carry

            lax.fori_loop(0, per_half, one_head, 0)

        for s in range(2):
            ks = slice(s * span, (s + 1) * span)
            dk_ref[s, q0 : q0 + span, :] += mm(ds_scr[ks, :], qm_scr[...])
            dv_ref[s, q0 : q0 + span, :] += mm(p_scr[ks, :], dom_scr[...])


def attention(bias, q, qt, do, dot, k, v, kt, vt):
    tokens, width = q.shape
    ext = k.shape[1]
    nq = QBLK * COLS
    keys = 2 * (QBLK + 2 * WMAX) * COLS
    vm = pl.BlockSpec(memory_space=pltpu.VMEM)
    return pl.pallas_call(
        attention_kernel,
        out_shape=(
            jax.ShapeDtypeStruct((width, tokens), BF),
            jax.ShapeDtypeStruct((width, tokens), F32),
            jax.ShapeDtypeStruct((2, ext, width), F32),
            jax.ShapeDtypeStruct((2, ext, width), F32),
        ),
        in_specs=[vm] * 9,
        out_specs=(vm,) * 4,
        scratch_shapes=[
            pltpu.VMEM((keys, nq), F32),
            pltpu.VMEM((keys, nq), F32),
            pltpu.VMEM((keys, HEADS * nq), BF),
            pltpu.VMEM((keys, HEADS * nq), BF),
            pltpu.VMEM((HEADS * nq, width), BF),
            pltpu.VMEM((HEADS * nq, width), BF),
        ],
        compiler_params=pltpu.CompilerParams(vmem_limit_bytes=48 << 20),
        cost_estimate=pl.CostEstimate(
            flops=int(2e10), bytes_accessed=int(8e6), transcendentals=int(4e6)
        ),
        name="attention",
    )(bias, q, qt, do, dot, k, v, kt, vt)


def shifted(array, axis, by):
    devices = lax.axis_size(axis)
    pairs = [(i, i + by) for i in range(devices) if 0 <= i + by < devices]
    return lax.ppermute(array, axis, pairs)


def from_partner(value):
    return lax.ppermute(value, "row", [(0, 1), (1, 0)])


def row_halo(array, row_id, width):
    length = array.shape[-3]
    first = lax.slice_in_dim(array, 0, width, axis=array.ndim - 3)
    last = lax.slice_in_dim(array, length - width, length, axis=array.ndim - 3)
    got = from_partner(jnp.where(row_id == 0, last, first))
    zero = jnp.zeros_like(got)
    before = jnp.where(row_id == 0, zero, got)
    after = jnp.where(row_id == 0, got, zero)
    return jnp.concatenate([before, array, after], axis=array.ndim - 3)


def local(
    latents, ref_frames, windows, quant_level, quant_scale,
    shared_proj, value_proj, output_proj, conv_taps, cotangent,
):
    width = latents.shape[2]
    rows_dev = latents.shape[1] // COLS
    row_devs = lax.axis_size("row")
    total_rows = rows_dev * row_devs
    frame_id = lax.axis_index("frame")
    row_id = lax.axis_index("row")
    own_refs = ref_frames[0]
    window = windows[0]
    ext_rows = rows_dev + 2 * WMAX
    offsets = [d * (1 << level) for level in range(LEVELS) for d in (1, -1)]
    grid = (rows_dev, COLS, width)
    tokens = latents[0]
    token_grid = tokens.reshape(grid)

    slot = jnp.zeros((2,) + grid, BF)
    for offset in offsets:
        arrived = shifted(token_grid, "frame", offset)
        matched = (own_refs == frame_id - offset).reshape(2, 1, 1, 1)
        slot = jnp.where(matched, arrived[None], slot)
    slot_ext = row_halo(slot, row_id, WMAX)
    slot_flat = slot_ext.reshape(2, ext_rows * COLS, width)
    q = mm(tokens, shared_proj).astype(BF)
    qt = mm(shared_proj, tokens, 0, 1).astype(BF)
    k = mm(slot_flat, shared_proj, 2, 0).astype(BF)
    v = mm(slot_flat, value_proj, 2, 0).astype(BF)
    kt = jnp.transpose(k, (0, 2, 1))
    vt = jnp.transpose(v, (0, 2, 1))

    levels = jnp.arange(quant_scale.shape[0], dtype=jnp.int32)
    gain = jnp.sum(jnp.where((levels == quant_level[0])[:, None], quant_scale, 0.0), axis=0)[None]
    grad_z = cotangent[0].astype(F32) * gain
    grad_zb = grad_z.astype(BF)
    grad_ext = row_halo(grad_zb.reshape(grid), row_id, 1).reshape(-1, width)
    grad_resid = grad_z
    for t in range(3):
        part = grad_ext[(2 - t) * COLS : (2 - t + rows_dev) * COLS]
        grad_resid = grad_resid + mm(part, conv_taps[t], 1, 1)
    grad_rb = grad_resid.astype(BF)
    do = mm(grad_rb, output_proj, 1, 1).astype(BF)
    dot = jnp.transpose(do)

    blocks = rows_dev // QBLK
    span_rows = QBLK + 2 * WMAX
    b_i = jnp.arange(blocks, dtype=jnp.int32)[:, None, None]
    r_i = jnp.arange(span_rows, dtype=jnp.int32)[None, :, None]
    i_i = (jnp.arange(QBLK * COLS, dtype=jnp.int32) // COLS)[None, None, :]
    key_row = row_id * rows_dev + b_i * QBLK + r_i - WMAX
    allowed = (jnp.abs(r_i - WMAX - i_i) <= window) & (key_row >= 0) & (key_row < total_rows)
    bias = jnp.where(allowed, 0.0, -jnp.inf).astype(F32)

    mixt, dqt, dk, dv = attention(bias, q, qt, do, dot, k, v, kt, vt)

    residual = tokens.astype(F32) + mm(mixt, output_proj, 0, 0)
    hidden_ext = row_halo(residual.astype(BF).reshape(grid), row_id, 1).reshape(-1, width)
    context = residual
    for t in range(3):
        context = context + mm(hidden_ext[t * COLS : (t + rows_dev) * COLS], conv_taps[t])
    coded = (context * gain).astype(BF)

    dkb = dk.astype(BF)
    dvb = dv.astype(BF)
    partial = (mm(dkb, shared_proj, 2, 1) + mm(dvb, value_proj, 2, 1)).reshape(
        2, ext_rows, COLS, width
    )
    upper = partial[:, :WMAX]
    lower = partial[:, WMAX + rows_dev :]
    got = from_partner(jnp.where(row_id == 0, lower, upper).astype(BF)).astype(F32)
    filler = jnp.zeros((2, rows_dev - WMAX, COLS, width), F32)
    middle = (
        partial[:, WMAX : WMAX + rows_dev]
        + jnp.concatenate([jnp.where(row_id == 0, 0.0, got), filler], axis=1)
        + jnp.concatenate([filler, jnp.where(row_id == 0, got, 0.0)], axis=1)
    )
    grad_latents = grad_resid + mm(dqt.astype(BF), shared_proj, 0, 1)
    for offset in offsets:
        matched = (own_refs == frame_id - offset).reshape(2, 1, 1, 1)
        outgoing = jnp.sum(jnp.where(matched, middle, 0.0), axis=0).astype(BF)
        grad_latents = grad_latents + shifted(outgoing, "frame", -offset).astype(F32).reshape(
            -1, width
        )

    flat = slot_flat.reshape(-1, width)
    grad_shared = mm(tokens, dqt.astype(BF), 0, 1) + mm(flat, dkb.reshape(-1, width), 0, 0)
    grad_values = mm(flat, dvb.reshape(-1, width), 0, 0)
    grad_output = mm(mixt, grad_rb)
    grad_taps = jnp.stack(
        [mm(hidden_ext[t * COLS : (t + rows_dev) * COLS], grad_zb, 0, 0) for t in range(3)]
    )
    sums = lax.psum((grad_shared, grad_values, grad_output, grad_taps), ("frame", "row"))
    norm = 1.0 / math.sqrt(lax.axis_size("frame") * total_rows * COLS)
    return (
        coded[None],
        grad_latents.astype(BF)[None],
        *(total * norm for total in sums),
    )


def solution(mesh):
    tok = P(("groups", "frame"), "row", None)
    frm = P(("groups", "frame"))
    placed = (tok, P(("groups", "frame"), None), frm, frm, P(), P(), P(), P(), P(), tok)
    return jax.shard_map(
        local,
        mesh=mesh,
        in_specs=placed,
        out_specs=(
            tok, tok, P("groups", None), P("groups", None), P("groups", None),
            P("groups", None, None),
        ),
        check_vma=False,
    )
```

```python
import functools
import math

import jax
import jax.numpy as jnp
from jax import lax
from jax.experimental import pallas as pl
from jax.experimental.pallas import tpu as pltpu
from jax.sharding import PartitionSpec as P

HEADS = 8
DH = 32
COLS = 64
QBLK = 4
WMAX = 2

SCORE_SCALE = 1.5 / math.sqrt(DH)
LOG2E = math.log2(math.e)
BF = jnp.bfloat16
F32 = jnp.float32


def mm(a, b, ca=1, cb=0):
    return lax.dot_general(a, b, (((ca,), (cb,)), ((), ())), preferred_element_type=F32)


def attention_kernel(
    bias_ref, q_ref, qt_ref, do_ref, dot_ref, k_ref, v_ref, kt_ref, vt_ref,
    mixt_ref, dqt_ref, dk_ref, dv_ref,
    s_scr, dp_scr, p_scr, ds_scr, qm_scr, dom_scr,
):
    tokens, width = q_ref.shape
    nq = QBLK * COLS
    span = (QBLK + 2 * WMAX) * COLS
    rows = span // COLS
    blocks = tokens // nq
    half = width // 2
    per_half = HEADS // 2
    lane = lax.broadcasted_iota(jnp.int32, (1, width), 1) // DH
    sub = lax.broadcasted_iota(jnp.int32, (half, 1), 0) // DH

    dk_ref[...] = jnp.zeros_like(dk_ref)
    dv_ref[...] = jnp.zeros_like(dv_ref)

    for b in range(blocks):
        q0 = b * nq
        qb = q_ref[q0 : q0 + nq, :]
        dob = do_ref[q0 : q0 + nq, :]
        for h in range(HEADS):
            keep = lane == h
            qm_scr[h * nq : (h + 1) * nq, :] = jnp.where(keep, qb, jnp.zeros_like(qb))
            dom_scr[h * nq : (h + 1) * nq, :] = jnp.where(keep, dob, jnp.zeros_like(dob))

        for hf in range(2):
            f0 = hf * half
            qth = qt_ref[f0 : f0 + half, q0 : q0 + nq]
            doth = dot_ref[f0 : f0 + half, q0 : q0 + nq]

            def one_head(hh, carry, hf=hf, f0=f0, qth=qth, doth=doth, q0=q0, b=b):
                keep = sub == hh
                qtm = jnp.where(keep, qth, jnp.zeros_like(qth))
                dotm = jnp.where(keep, doth, jnp.zeros_like(doth))
                for s in range(2):
                    s_scr[s * span : (s + 1) * span, :] = mm(
                        k_ref[s, q0 : q0 + span, f0 : f0 + half], qtm
                    )
                    dp_scr[s * span : (s + 1) * span, :] = mm(
                        v_ref[s, q0 : q0 + span, f0 : f0 + half], dotm
                    )
                m8 = jnp.full((8, nq), -jnp.inf, F32)
                for c in range(2 * rows):
                    x = s_scr[c * COLS : (c + 1) * COLS, :].reshape(COLS // 8, 8, nq)
                    m8 = jnp.maximum(m8, jnp.max(x, axis=0) + bias_ref[b, c % rows, :][None, :])
                m = jnp.max(m8, axis=0, keepdims=True)
                kk = SCORE_SCALE * LOG2E
                l8 = jnp.zeros((8, nq), F32)
                u8 = jnp.zeros((8, nq), F32)
                for c in range(2 * rows):
                    sl = slice(c * COLS, (c + 1) * COLS)
                    off = (bias_ref[b, c % rows, :][None, :] - m) * kk
                    p = jnp.exp2(s_scr[sl, :] * kk + off)
                    s_scr[sl, :] = p
                    l8 = l8 + jnp.sum(p.reshape(COLS // 8, 8, nq), axis=0)
                    u8 = u8 + jnp.sum((p * dp_scr[sl, :]).reshape(COLS // 8, 8, nq), axis=0)
                inv = 1.0 / jnp.sum(l8, axis=0, keepdims=True)
                ci = inv * SCORE_SCALE
                inner = jnp.sum(u8, axis=0, keepdims=True) * inv * ci
                col = pl.multiple_of((hf * per_half + hh) * nq, nq)
                for c in range(2 * rows):
                    sl = slice(c * COLS, (c + 1) * COLS)
                    p = s_scr[sl, :]
                    p_scr[sl, pl.ds(col, nq)] = (p * inv).astype(BF)
                    ds_scr[sl, pl.ds(col, nq)] = (p * (dp_scr[sl, :] * ci - inner)).astype(BF)
                r0 = pl.multiple_of(f0 + hh * DH, DH)
                mix = jnp.zeros((DH, nq), F32)
                dq = jnp.zeros((DH, nq), F32)
                for s in range(2):
                    ks = slice(s * span, (s + 1) * span)
                    mix = mix + mm(
                        vt_ref[s, pl.ds(r0, DH), q0 : q0 + span], p_scr[ks, pl.ds(col, nq)]
                    )
                    dq = dq + mm(
                        kt_ref[s, pl.ds(r0, DH), q0 : q0 + span], ds_scr[ks, pl.ds(col, nq)]
                    )
                mixt_ref[pl.ds(r0, DH), q0 : q0 + nq] = mix.astype(BF)
                dqt_ref[pl.ds(r0, DH), q0 : q0 + nq] = dq
                return carry

            lax.fori_loop(0, per_half, one_head, 0)

        for s in range(2):
            ks = slice(s * span, (s + 1) * span)
            dk_ref[s, q0 : q0 + span, :] += mm(ds_scr[ks, :], qm_scr[...])
            dv_ref[s, q0 : q0 + span, :] += mm(p_scr[ks, :], dom_scr[...])


def attention(bias, q, qt, do, dot, k, v, kt, vt):
    tokens, width = q.shape
    ext = k.shape[1]
    nq = QBLK * COLS
    keys = 2 * (QBLK + 2 * WMAX) * COLS
    vm = pl.BlockSpec(memory_space=pltpu.VMEM)
    return pl.pallas_call(
        attention_kernel,
        out_shape=(
            jax.ShapeDtypeStruct((width, tokens), BF),
            jax.ShapeDtypeStruct((width, tokens), F32),
            jax.ShapeDtypeStruct((2, ext, width), F32),
            jax.ShapeDtypeStruct((2, ext, width), F32),
        ),
        in_specs=[vm] * 9,
        out_specs=(vm,) * 4,
        scratch_shapes=[
            pltpu.VMEM((keys, nq), F32),
            pltpu.VMEM((keys, nq), F32),
            pltpu.VMEM((keys, HEADS * nq), BF),
            pltpu.VMEM((keys, HEADS * nq), BF),
            pltpu.VMEM((HEADS * nq, width), BF),
            pltpu.VMEM((HEADS * nq, width), BF),
        ],
        compiler_params=pltpu.CompilerParams(vmem_limit_bytes=48 << 20),
        cost_estimate=pl.CostEstimate(
            flops=int(2e10), bytes_accessed=int(8e6), transcendentals=int(4e6)
        ),
        name="attention",
    )(bias, q, qt, do, dot, k, v, kt, vt)


MESH = pl.DeviceIdType.MESH
CHUNKS = 4


def greet(targets):
    barrier = pltpu.get_barrier_semaphore()
    count = 0
    for exists, device in targets:

        @pl.when(exists)
        def _(device=device):
            pl.semaphore_signal(barrier, inc=1, device_id=device, device_id_type=MESH)

        count = count + jnp.where(exists, 1, 0)
    pl.semaphore_wait(barrier, count)


def fetch_kernel(frames, x_ref, ct_ref, buf_ref, halo_ref, cth_ref, ssem, rsem, hs, hr, cs, cr):
    f = lax.axis_index("frame")
    r = lax.axis_index("row")
    tokens = x_ref.shape[0]
    odd = lax.rem(f, 2)
    pair = f + 1 - 2 * odd
    lo2, hi2, lo4, hi4 = f >= 2, f + 2 < frames, f >= 4, f + 4 < frames
    side = ((odd == 1) & (f + 1 < frames)) | ((odd == 0) & (f >= 1))
    always = f >= 0
    have = (lo2, hi2, always, lo4, hi4, side)
    partner = {"row": 1 - r}
    up, down, across = {"frame": f + 2}, {"frame": f - 2}, {"frame": pair}
    greet(((hi2, up), (lo2, down), (always, across), (always, partner)))

    edge = ct_ref.shape[0] - COLS
    ct_copy = pltpu.make_async_remote_copy(
        ct_ref.at[pl.ds(pl.multiple_of((1 - r) * edge, COLS), COLS)], cth_ref, cs, cr,
        device_id=partner, device_id_type=MESH,
    )
    ct_copy.start()
    step = tokens // CHUNKS

    def copy(kind, c, source, device):
        part = pl.ds(c * step, step)
        return pltpu.make_async_remote_copy(
            source.at[part], buf_ref.at[kind, part], ssem.at[kind, c], rsem.at[kind, c],
            device_id=device, device_id_type=MESH,
        )

    for c in range(CHUNKS):

        @pl.when(hi2)
        def _():
            copy(0, c, x_ref, up).start()

        @pl.when(lo2)
        def _():
            copy(1, c, x_ref, down).start()

        copy(2, c, x_ref, across).start()

    for c in range(CHUNKS):

        @pl.when(lo2)
        def _():
            copy(0, c, x_ref, across).wait_recv()

        @pl.when(lo2 & hi2)
        def _():
            copy(3, c, buf_ref.at[0], up).start()

        @pl.when(lo2 & (odd == 1))
        def _():
            copy(5, c, buf_ref.at[0], across).start()

        @pl.when(hi2)
        def _():
            copy(1, c, x_ref, across).wait_recv()

        @pl.when(hi2 & lo2)
        def _():
            copy(4, c, buf_ref.at[1], down).start()

        @pl.when(hi2 & (odd == 0))
        def _():
            copy(5, c, buf_ref.at[1], across).start()

    rim = WMAX * COLS
    start = pl.multiple_of((1 - r) * (tokens - rim), rim)

    def halo(kind):
        return pltpu.make_async_remote_copy(
            buf_ref.at[kind, pl.ds(start, rim)], halo_ref.at[kind], hs.at[kind], hr.at[kind],
            device_id=partner, device_id_type=MESH,
        )

    for kind in range(6):

        @pl.when(have[kind])
        def _():
            if kind > 1:
                for c in range(CHUNKS):
                    copy(kind, c, x_ref, across).wait_recv()
            halo(kind).start()

    sent = (hi2, lo2, always, lo2 & hi2, lo2 & hi2, (lo2 & (odd == 1)) | (hi2 & (odd == 0)))
    for kind in range(6):

        @pl.when(have[kind])
        def _():
            halo(kind).wait()

        @pl.when(sent[kind])
        def _():
            for c in range(CHUNKS):
                copy(kind, c, x_ref, across).wait_send()

    ct_copy.wait()


def fetch(tokens, cotangent, frames):
    count, width = tokens.shape
    vm = pl.BlockSpec(memory_space=pltpu.VMEM)
    dma = pltpu.SemaphoreType.DMA
    return pl.pallas_call(
        functools.partial(fetch_kernel, frames),
        out_shape=(
            jax.ShapeDtypeStruct((6, count, width), BF),
            jax.ShapeDtypeStruct((6, WMAX * COLS, width), BF),
            jax.ShapeDtypeStruct((COLS, width), BF),
        ),
        in_specs=[vm] * 2,
        out_specs=(vm,) * 3,
        scratch_shapes=[
            dma((6, CHUNKS)), dma((6, CHUNKS)), dma((6,)), dma((6,)), dma(()), dma(()),
        ],
        compiler_params=pltpu.CompilerParams(collective_id=0, has_side_effects=True),
        name="fetch",
    )(tokens, cotangent)


def reduce_kernel(
    frames, out_ref, base_ref, w_ref, lat_ref, wsum_ref,
    rb, sb, wp, ws, wr, ssem, rsem, ps, pr, rs_s, rs_r, ag_s, ag_r, fw_s, fw_r,
):
    f = lax.axis_index("frame")
    r = lax.axis_index("row")
    tokens = base_ref.shape[0]
    odd = lax.rem(f, 2)
    pair = f + 1 - 2 * odd
    lo2, hi2, lo4, hi4 = f >= 2, f + 2 < frames, f >= 4, f + 4 < frames
    always = f >= 0
    side = ((odd == 1) & (f + 1 < frames)) | ((odd == 0) & (f >= 1))
    relay = ((odd == 1) & lo2) | ((odd == 0) & hi2)
    partner = {"row": 1 - r}
    up, down, across = {"frame": f + 2}, {"frame": f - 2}, {"frame": pair}

    barrier = pltpu.get_barrier_semaphore()
    pl.semaphore_signal(barrier, inc=1, device_id=partner, device_id_type=MESH)

    def hello(k, carry):
        pl.semaphore_signal(
            barrier, inc=1, device_id={"frame": lax.rem(f + k, frames)}, device_id_type=MESH
        )
        return carry

    lax.fori_loop(1, frames, hello, 0)
    pl.semaphore_wait(barrier, frames)

    step = tokens // CHUNKS
    sent = (hi2, lo2, always, hi4, lo4, side)
    got = (lo2, hi2, always, lo2 & hi2, lo2 & hi2, relay)
    device = (up, down, across, up, down, across)

    def copy(kind, c, source):
        part = pl.ds(c * step, step)
        return pltpu.make_async_remote_copy(
            source.at[part], rb.at[kind, part], ssem.at[kind, c], rsem.at[kind, c],
            device_id=device[kind], device_id_type=MESH,
        )

    halves = pltpu.make_async_remote_copy(
        w_ref.at[1 - r], wp, ps, pr, device_id=partner, device_id_type=MESH
    )
    halves.start()
    for c in range(CHUNKS):
        for kind in (3, 4, 5):

            @pl.when(sent[kind])
            def _():
                copy(kind, c, out_ref.at[kind]).start()

    for kind in (0, 1, 3, 4, 5):

        @pl.when(jnp.logical_not(got[kind]))
        def _():
            rb[kind, :, :] = jnp.zeros((tokens, rb.shape[2]), BF)

    halves.wait()
    ws[...] = (w_ref[r] + wp[...]).astype(BF)

    def piece(ref, mine, other, target, s_sem, r_sem, slot, k):
        return pltpu.make_async_remote_copy(
            mine, other, s_sem.at[k], r_sem.at[slot],
            device_id={"frame": target}, device_id_type=MESH,
        )

    def scatter(k):
        target = lax.rem(f + k, frames)
        return piece(ws, ws.at[target], wr.at[f], target, rs_s, rs_r, f, k)

    def arrived(k):
        source = lax.rem(f - k + frames, frames)
        return source, piece(ws, ws.at[source], wr.at[source], source, rs_s, rs_r, source, k)

    def gather(k):
        target = lax.rem(f + k, frames)
        return piece(ws, wsum_ref.at[r, f], wsum_ref.at[r, f], target, ag_s, ag_r, f, k)

    def gathered(k):
        source = lax.rem(f - k + frames, frames)
        return source, piece(
            ws, wsum_ref.at[r, source], wsum_ref.at[r, source], source, ag_s, ag_r, source, k
        )

    def forward(j, own):
        return pltpu.make_async_remote_copy(
            wsum_ref.at[own, j], wsum_ref.at[own, j], fw_s.at[j], fw_r.at[j],
            device_id=partner, device_id_type=MESH,
        )

    def run(body):
        lax.fori_loop(1, frames, lambda k, carry: (body(k), carry)[1], 0)

    run(lambda k: scatter(k).start())
    for c in range(CHUNKS):
        copy(2, c, out_ref.at[2]).start()

    even = jnp.where(odd == 0, 1.0, 0.0).astype(F32)
    for c in range(CHUNKS):
        part = slice(c * step, (c + 1) * step)
        for kind in (3, 4, 5):

            @pl.when(got[kind])
            def _():
                copy(kind, c, out_ref.at[kind]).wait_recv()

        extra = rb[5, part, :].astype(F32)
        rising = out_ref[0, part, :].astype(F32) + rb[3, part, :].astype(F32) + extra * even
        falling = (
            out_ref[1, part, :].astype(F32) + rb[4, part, :].astype(F32) + extra * (1.0 - even)
        )
        sb[0, part, :] = rising.astype(BF)
        sb[1, part, :] = falling.astype(BF)

        @pl.when(hi2)
        def _():
            copy(0, c, sb.at[0]).start()

        @pl.when(lo2)
        def _():
            copy(1, c, sb.at[1]).start()

    def add_piece(k, total):
        source, waiting = arrived(k)
        waiting.wait_recv()
        return total + wr[source].astype(F32)

    total = lax.fori_loop(1, frames, add_piece, w_ref[r, f] + wp[f])
    wsum_ref[r, f] = total.astype(BF)
    run(lambda k: gather(k).start())
    forward(f, r).start()

    for c in range(CHUNKS):
        part = slice(c * step, (c + 1) * step)
        for kind in (0, 1, 2):

            @pl.when(got[kind])
            def _():
                copy(kind, c, out_ref.at[kind]).wait_recv()

        lat_ref[part, :] = (
            base_ref[part, :]
            + rb[0, part, :].astype(F32)
            + rb[1, part, :].astype(F32)
            + rb[2, part, :].astype(F32)
        ).astype(BF)

    def pass_on(k):
        source, waiting = gathered(k)
        waiting.wait_recv()
        forward(source, r).start()

    run(pass_on)

    def finish(k):
        scatter(k).wait_send()
        gather(k).wait_send()

    run(finish)

    def last(j, carry):
        forward(j, r).wait_send()
        forward(j, 1 - r).wait_recv()
        return carry

    lax.fori_loop(0, frames, last, 0)
    for kind in range(6):

        @pl.when(sent[kind])
        def _():
            for c in range(CHUNKS):
                copy(kind, c, out_ref.at[kind]).wait_send()


def reduce(outgoing, base, grads, frames):
    count, width = base.shape
    vm = pl.BlockSpec(memory_space=pltpu.VMEM)
    dma = pltpu.SemaphoreType.DMA
    pieces = grads.shape[1:]
    return pl.pallas_call(
        functools.partial(reduce_kernel, frames),
        out_shape=(
            jax.ShapeDtypeStruct((count, width), BF),
            jax.ShapeDtypeStruct(grads.shape, BF),
        ),
        in_specs=[vm] * 3,
        out_specs=(vm,) * 2,
        scratch_shapes=[
            pltpu.VMEM((6, count, width), BF),
            pltpu.VMEM((2, count, width), BF),
            pltpu.VMEM(pieces, F32),
            pltpu.VMEM(pieces, BF),
            pltpu.VMEM(pieces, BF),
            dma((6, CHUNKS)), dma((6, CHUNKS)), dma(()), dma(()),
            dma((frames,)), dma((frames,)), dma((frames,)), dma((frames,)),
            dma((frames,)), dma((frames,)),
        ],
        compiler_params=pltpu.CompilerParams(collective_id=1, has_side_effects=True),
        name="reduce",
    )(outgoing, base, grads)


def from_partner(value):
    return lax.ppermute(value, "row", [(0, 1), (1, 0)])


def row_halo(array, row_id, width):
    length = array.shape[-3]
    first = lax.slice_in_dim(array, 0, width, axis=array.ndim - 3)
    last = lax.slice_in_dim(array, length - width, length, axis=array.ndim - 3)
    got = from_partner(jnp.where(row_id == 0, last, first))
    zero = jnp.zeros_like(got)
    before = jnp.where(row_id == 0, zero, got)
    after = jnp.where(row_id == 0, got, zero)
    return jnp.concatenate([before, array, after], axis=array.ndim - 3)


def local(
    latents, ref_frames, windows, quant_level, quant_scale,
    shared_proj, value_proj, output_proj, conv_taps, cotangent,
):
    width = latents.shape[2]
    rows_dev = latents.shape[1] // COLS
    row_devs = lax.axis_size("row")
    total_rows = rows_dev * row_devs
    frame_id = lax.axis_index("frame")
    row_id = lax.axis_index("row")
    own_refs = ref_frames[0]
    window = windows[0]
    ext_rows = rows_dev + 2 * WMAX
    grid = (rows_dev, COLS, width)
    tokens = latents[0]
    frames = lax.axis_size("frame")
    odd = frame_id % 2
    sources = (
        frame_id - 2, frame_id + 2, frame_id + 1 - 2 * odd,
        frame_id - 4, frame_id + 4, frame_id - 1 + 2 * odd,
    )
    buf, halo, ct_edge = fetch(tokens, cotangent[0], frames)
    slot = jnp.zeros((2,) + tokens.shape, BF)
    rim = jnp.zeros((2, WMAX * COLS, width), BF)
    for kind, source in enumerate(sources):
        matched = (own_refs == source).reshape(2, 1, 1)
        slot = jnp.where(matched, buf[kind][None], slot)
        rim = jnp.where(matched, halo[kind][None], rim)
    zero = jnp.zeros_like(rim)
    slot_ext = jnp.concatenate(
        [jnp.where(row_id == 0, zero, rim), slot, jnp.where(row_id == 0, rim, zero)], axis=1
    )
    slot_flat = slot_ext.reshape(2, ext_rows * COLS, width)
    q = mm(tokens, shared_proj).astype(BF)
    qt = mm(shared_proj, tokens, 0, 1).astype(BF)
    k = mm(slot_flat, shared_proj, 2, 0).astype(BF)
    v = mm(slot_flat, value_proj, 2, 0).astype(BF)
    kt = jnp.transpose(k, (0, 2, 1))
    vt = jnp.transpose(v, (0, 2, 1))

    levels = jnp.arange(quant_scale.shape[0], dtype=jnp.int32)
    gain = jnp.sum(jnp.where((levels == quant_level[0])[:, None], quant_scale, 0.0), axis=0)[None]
    grad_z = cotangent[0].astype(F32) * gain
    grad_zb = grad_z.astype(BF)
    edge = (ct_edge.astype(F32) * gain).astype(BF)
    blank = jnp.zeros_like(edge)
    grad_ext = jnp.concatenate(
        [jnp.where(row_id == 0, blank, edge), grad_zb, jnp.where(row_id == 0, edge, blank)], axis=0
    )
    grad_resid = grad_z
    for t in range(3):
        part = grad_ext[(2 - t) * COLS : (2 - t + rows_dev) * COLS]
        grad_resid = grad_resid + mm(part, conv_taps[t], 1, 1)
    grad_rb = grad_resid.astype(BF)
    do = mm(grad_rb, output_proj, 1, 1).astype(BF)
    dot = jnp.transpose(do)

    blocks = rows_dev // QBLK
    span_rows = QBLK + 2 * WMAX
    b_i = jnp.arange(blocks, dtype=jnp.int32)[:, None, None]
    r_i = jnp.arange(span_rows, dtype=jnp.int32)[None, :, None]
    i_i = (jnp.arange(QBLK * COLS, dtype=jnp.int32) // COLS)[None, None, :]
    key_row = row_id * rows_dev + b_i * QBLK + r_i - WMAX
    allowed = (jnp.abs(r_i - WMAX - i_i) <= window) & (key_row >= 0) & (key_row < total_rows)
    bias = jnp.where(allowed, 0.0, -jnp.inf).astype(F32)

    mixt, dqt, dk, dv = attention(bias, q, qt, do, dot, k, v, kt, vt)

    residual = tokens.astype(F32) + mm(mixt, output_proj, 0, 0)
    hidden_ext = row_halo(residual.astype(BF).reshape(grid), row_id, 1).reshape(-1, width)
    context = residual
    for t in range(3):
        context = context + mm(hidden_ext[t * COLS : (t + rows_dev) * COLS], conv_taps[t])
    coded = (context * gain).astype(BF)

    dkb = dk.astype(BF)
    dvb = dv.astype(BF)
    partial = (mm(dkb, shared_proj, 2, 1) + mm(dvb, value_proj, 2, 1)).reshape(
        2, ext_rows, COLS, width
    )
    upper = partial[:, :WMAX]
    lower = partial[:, WMAX + rows_dev :]
    got = from_partner(jnp.where(row_id == 0, lower, upper).astype(BF)).astype(F32)
    filler = jnp.zeros((2, rows_dev - WMAX, COLS, width), F32)
    middle = (
        partial[:, WMAX : WMAX + rows_dev]
        + jnp.concatenate([jnp.where(row_id == 0, 0.0, got), filler], axis=1)
        + jnp.concatenate([filler, jnp.where(row_id == 0, got, 0.0)], axis=1)
    )
    grad_latents = grad_resid + mm(dqt.astype(BF), shared_proj, 0, 1)
    targets = (
        frame_id + 2, frame_id - 2, frame_id + 1 - 2 * odd,
        frame_id + 4, frame_id - 4, frame_id - 1 + 2 * odd,
    )
    outgoing = jnp.stack(
        [
            jnp.sum(jnp.where((own_refs == t).reshape(2, 1, 1, 1), middle, 0.0), axis=0)
            .astype(BF)
            .reshape(-1, width)
            for t in targets
        ]
    )
    flat = slot_flat.reshape(-1, width)
    grad_shared = mm(tokens, dqt.astype(BF), 0, 1) + mm(flat, dkb.reshape(-1, width), 0, 0)
    grad_values = mm(flat, dvb.reshape(-1, width), 0, 0)
    grad_output = mm(mixt, grad_rb)
    grad_taps = jnp.stack(
        [mm(hidden_ext[t * COLS : (t + rows_dev) * COLS], grad_zb, 0, 0) for t in range(3)]
    )
    stacked = jnp.concatenate(
        [grad_shared, grad_values, grad_output, grad_taps.reshape(-1, width)], axis=0
    )
    grads = stacked.reshape(2, frames, stacked.shape[0] // (2 * frames), width)
    new_latents, summed = reduce(outgoing, grad_latents, grads, frames)
    norm = 1.0 / math.sqrt(frames * total_rows * COLS)
    summed = summed.reshape(-1, width).astype(F32) * norm
    return (
        coded[None],
        new_latents[None],
        summed[:width],
        summed[width : 2 * width],
        summed[2 * width : 3 * width],
        summed[3 * width :].reshape(3, width, width),
    )


def solution(mesh):
    tok = P(("groups", "frame"), "row", None)
    frm = P(("groups", "frame"))
    placed = (tok, P(("groups", "frame"), None), frm, frm, P(), P(), P(), P(), P(), tok)
    return jax.shard_map(
        local,
        mesh=mesh,
        in_specs=placed,
        out_specs=(
            tok, tok, P("groups", None), P("groups", None), P("groups", None),
            P("groups", None, None),
        ),
        check_vma=False,
    )
```

```python
import functools
import math

import jax
import jax.numpy as jnp
from jax import lax
from jax.experimental import pallas as pl
from jax.experimental.pallas import tpu as pltpu
from jax.sharding import PartitionSpec as P

HEADS = 8
DH = 32
COLS = 64
QBLK = 4
WMAX = 2

SCORE_SCALE = 1.5 / math.sqrt(DH)
LOG2E = math.log2(math.e)
BF = jnp.bfloat16
F32 = jnp.float32


def mm(a, b, ca=1, cb=0):
    return lax.dot_general(a, b, (((ca,), (cb,)), ((), ())), preferred_element_type=F32)


def attention_kernel(
    meta_ref, buf_ref, halo_ref, x_ref, q_ref, qt_ref, do_ref, dot_ref, resid_ref,
    sp_ref, vp_ref, op_ref,
    residual_ref, hidden_ref, base_ref, part_ref, gs_ref, gv_ref, go_ref,
    xs_ref, k_ref, v_ref, kt_ref, vt_ref, mixt_ref, dqt_ref, dk_ref, dv_ref,
    s_scr, dp_scr, p_scr, ds_scr, qm_scr, dom_scr,
):
    tokens, width = q_ref.shape
    nq = QBLK * COLS
    span = (QBLK + 2 * WMAX) * COLS
    rows = span // COLS
    blocks = tokens // nq
    half = width // 2
    per_half = HEADS // 2
    lane = lax.broadcasted_iota(jnp.int32, (1, width), 1) // DH
    sub = lax.broadcasted_iota(jnp.int32, (half, 1), 0) // DH

    dk_ref[...] = jnp.zeros_like(dk_ref)
    dv_ref[...] = jnp.zeros_like(dv_ref)
    rim = WMAX * COLS
    window = meta_ref[2]
    row_id = meta_ref[3]
    first_row = row_id * (tokens // COLS)
    total_rows = meta_ref[4]
    zero_rim = jnp.zeros((rim, width), BF)
    for s in range(2):
        kind = meta_ref[s]
        xs_ref[s, rim : rim + tokens, :] = buf_ref[kind]

        @pl.when(row_id == 0)
        def _():
            xs_ref[s, :rim, :] = zero_rim
            xs_ref[s, rim + tokens :, :] = halo_ref[kind]

        @pl.when(row_id != 0)
        def _():
            xs_ref[s, :rim, :] = halo_ref[kind]
            xs_ref[s, rim + tokens :, :] = zero_rim

        xs = xs_ref[s]
        keys = mm(xs, sp_ref[...]).astype(BF)
        vals = mm(xs, vp_ref[...]).astype(BF)
        k_ref[s] = keys
        v_ref[s] = vals
        kt_ref[s] = keys.T
        vt_ref[s] = vals.T
    query_row = lax.broadcasted_iota(jnp.int32, (1, nq), 1) // COLS

    def bias_row(b, c):
        key_row = first_row + b * QBLK + c - WMAX
        reach = jnp.where((key_row >= 0) & (key_row < total_rows), window, -1)
        return jnp.where(jnp.abs(c - WMAX - query_row) <= reach, 0.0, -jnp.inf).astype(F32)

    for b in range(blocks):
        q0 = b * nq
        qb = q_ref[q0 : q0 + nq, :]
        dob = do_ref[q0 : q0 + nq, :]
        for h in range(HEADS):
            keep = lane == h
            qm_scr[h * nq : (h + 1) * nq, :] = jnp.where(keep, qb, jnp.zeros_like(qb))
            dom_scr[h * nq : (h + 1) * nq, :] = jnp.where(keep, dob, jnp.zeros_like(dob))

        for hf in range(2):
            f0 = hf * half
            qth = qt_ref[f0 : f0 + half, q0 : q0 + nq]
            doth = dot_ref[f0 : f0 + half, q0 : q0 + nq]

            def one_head(hh, carry, hf=hf, f0=f0, qth=qth, doth=doth, q0=q0, b=b):
                keep = sub == hh
                qtm = jnp.where(keep, qth, jnp.zeros_like(qth))
                dotm = jnp.where(keep, doth, jnp.zeros_like(doth))
                for s in range(2):
                    s_scr[s * span : (s + 1) * span, :] = mm(
                        k_ref[s, q0 : q0 + span, f0 : f0 + half], qtm
                    )
                    dp_scr[s * span : (s + 1) * span, :] = mm(
                        v_ref[s, q0 : q0 + span, f0 : f0 + half], dotm
                    )
                m8 = jnp.full((8, nq), -jnp.inf, F32)
                for c in range(2 * rows):
                    x = s_scr[c * COLS : (c + 1) * COLS, :].reshape(COLS // 8, 8, nq)
                    m8 = jnp.maximum(m8, jnp.max(x, axis=0) + bias_row(b, c % rows))
                m = jnp.max(m8, axis=0, keepdims=True)
                kk = SCORE_SCALE * LOG2E
                l8 = jnp.zeros((8, nq), F32)
                u8 = jnp.zeros((8, nq), F32)
                for c in range(2 * rows):
                    sl = slice(c * COLS, (c + 1) * COLS)
                    off = (bias_row(b, c % rows) - m) * kk
                    p = jnp.exp2(s_scr[sl, :] * kk + off)
                    s_scr[sl, :] = p
                    l8 = l8 + jnp.sum(p.reshape(COLS // 8, 8, nq), axis=0)
                    u8 = u8 + jnp.sum((p * dp_scr[sl, :]).reshape(COLS // 8, 8, nq), axis=0)
                inv = 1.0 / jnp.sum(l8, axis=0, keepdims=True)
                ci = inv * SCORE_SCALE
                inner = jnp.sum(u8, axis=0, keepdims=True) * inv * ci
                col = pl.multiple_of((hf * per_half + hh) * nq, nq)
                for c in range(2 * rows):
                    sl = slice(c * COLS, (c + 1) * COLS)
                    p = s_scr[sl, :]
                    p_scr[sl, pl.ds(col, nq)] = (p * inv).astype(BF)
                    ds_scr[sl, pl.ds(col, nq)] = (p * (dp_scr[sl, :] * ci - inner)).astype(BF)
                r0 = pl.multiple_of(f0 + hh * DH, DH)
                mix = jnp.zeros((DH, nq), F32)
                dq = jnp.zeros((DH, nq), F32)
                for s in range(2):
                    ks = slice(s * span, (s + 1) * span)
                    mix = mix + mm(
                        vt_ref[s, pl.ds(r0, DH), q0 : q0 + span], p_scr[ks, pl.ds(col, nq)]
                    )
                    dq = dq + mm(
                        kt_ref[s, pl.ds(r0, DH), q0 : q0 + span], ds_scr[ks, pl.ds(col, nq)]
                    )
                mixt_ref[pl.ds(r0, DH), q0 : q0 + nq] = mix.astype(BF)
                dqt_ref[pl.ds(r0, DH), q0 : q0 + nq] = dq
                return carry

            lax.fori_loop(0, per_half, one_head, 0)

        for s in range(2):
            ks = slice(s * span, (s + 1) * span)
            dk_ref[s, q0 : q0 + span, :] += mm(ds_scr[ks, :], qm_scr[...])
            dv_ref[s, q0 : q0 + span, :] += mm(p_scr[ks, :], dom_scr[...])

    dq = dqt_ref[...].T.astype(BF)
    base_ref[...] = resid_ref[...] + mm(dq, sp_ref[...], 1, 1)
    mixt = mixt_ref[...]
    go_ref[...] = mm(mixt, resid_ref[...].astype(BF))
    residual = x_ref[...].astype(F32) + mm(mixt.T, op_ref[...])
    residual_ref[...] = residual
    hidden_ref[...] = residual.astype(BF)
    gs = mm(x_ref[...].T, dq)
    gv = jnp.zeros((width, width), F32)
    for s in range(2):
        dk = dk_ref[s].astype(BF)
        dv = dv_ref[s].astype(BF)
        part_ref[s] = mm(dk, sp_ref[...], 1, 1) + mm(dv, vp_ref[...], 1, 1)
        xst = xs_ref[s].T
        gs = gs + mm(xst, dk)
        gv = gv + mm(xst, dv)
    gs_ref[...] = gs
    gv_ref[...] = gv


def attention(meta, buf, halo, x, q, qt, do, dot, resid, shared, value, output):
    tokens, width = q.shape
    ext = tokens + 2 * WMAX * COLS
    nq = QBLK * COLS
    keys = 2 * (QBLK + 2 * WMAX) * COLS
    vm = pl.BlockSpec(memory_space=pltpu.VMEM)
    full = jax.ShapeDtypeStruct((tokens, width), F32)
    square = jax.ShapeDtypeStruct((width, width), F32)
    return pl.pallas_call(
        attention_kernel,
        out_shape=(
            full,
            jax.ShapeDtypeStruct((tokens, width), BF),
            full,
            jax.ShapeDtypeStruct((2, ext, width), F32),
            square, square, square,
        ),
        in_specs=[pl.BlockSpec(memory_space=pltpu.SMEM)] + [vm] * 11,
        out_specs=(vm,) * 7,
        scratch_shapes=[
            pltpu.VMEM((2, ext, width), BF),
            pltpu.VMEM((2, ext, width), BF),
            pltpu.VMEM((2, ext, width), BF),
            pltpu.VMEM((2, width, ext), BF),
            pltpu.VMEM((2, width, ext), BF),
            pltpu.VMEM((width, tokens), BF),
            pltpu.VMEM((width, tokens), F32),
            pltpu.VMEM((2, ext, width), F32),
            pltpu.VMEM((2, ext, width), F32),
            pltpu.VMEM((keys, nq), F32),
            pltpu.VMEM((keys, nq), F32),
            pltpu.VMEM((keys, HEADS * nq), BF),
            pltpu.VMEM((keys, HEADS * nq), BF),
            pltpu.VMEM((HEADS * nq, width), BF),
            pltpu.VMEM((HEADS * nq, width), BF),
        ],
        compiler_params=pltpu.CompilerParams(vmem_limit_bytes=48 << 20),
        cost_estimate=pl.CostEstimate(
            flops=int(2e10), bytes_accessed=int(8e6), transcendentals=int(4e6)
        ),
        name="attention",
    )(meta, buf, halo, x, q, qt, do, dot, resid, shared, value, output)


MESH = pl.DeviceIdType.MESH
CHUNKS = 4


def greet(targets):
    barrier = pltpu.get_barrier_semaphore()
    count = 0
    for exists, device in targets:

        @pl.when(exists)
        def _(device=device):
            pl.semaphore_signal(barrier, inc=1, device_id=device, device_id_type=MESH)

        count = count + jnp.where(exists, 1, 0)
    pl.semaphore_wait(barrier, count)


def fetch_kernel(
    frames, level_ref, x_ref, ct_ref, qs_ref, sp_ref, op_ref, taps_ref,
    buf_ref, halo_ref, q_ref, qt_ref, do_ref, dot_ref, gzb_ref, resid_ref, gain_ref,
    cth_ref, ext_ref, ssem, rsem, hs, hr, cs, cr,
):
    f = lax.axis_index("frame")
    r = lax.axis_index("row")
    tokens = x_ref.shape[0]
    odd = lax.rem(f, 2)
    pair = f + 1 - 2 * odd
    lo2, hi2, lo4, hi4 = f >= 2, f + 2 < frames, f >= 4, f + 4 < frames
    side = ((odd == 1) & (f + 1 < frames)) | ((odd == 0) & (f >= 1))
    always = f >= 0
    have = (lo2, hi2, always, lo4, hi4, side)
    partner = {"row": 1 - r}
    up, down, across = {"frame": f + 2}, {"frame": f - 2}, {"frame": pair}
    greet(((hi2, up), (lo2, down), (always, across), (always, partner)))

    edge = ct_ref.shape[0] - COLS
    ct_copy = pltpu.make_async_remote_copy(
        ct_ref.at[pl.ds(pl.multiple_of((1 - r) * edge, COLS), COLS)], cth_ref, cs, cr,
        device_id=partner, device_id_type=MESH,
    )
    ct_copy.start()
    step = tokens // CHUNKS

    def copy(kind, c, source, device):
        part = pl.ds(c * step, step)
        return pltpu.make_async_remote_copy(
            source.at[part], buf_ref.at[kind, part], ssem.at[kind, c], rsem.at[kind, c],
            device_id=device, device_id_type=MESH,
        )

    for c in range(CHUNKS):

        @pl.when(hi2)
        def _():
            copy(0, c, x_ref, up).start()

        @pl.when(lo2)
        def _():
            copy(1, c, x_ref, down).start()

        copy(2, c, x_ref, across).start()

    for c in range(CHUNKS):

        @pl.when(lo2)
        def _():
            copy(0, c, x_ref, across).wait_recv()

        @pl.when(lo2 & hi2)
        def _():
            copy(3, c, buf_ref.at[0], up).start()

        @pl.when(lo2 & (odd == 1))
        def _():
            copy(5, c, buf_ref.at[0], across).start()

        @pl.when(hi2)
        def _():
            copy(1, c, x_ref, across).wait_recv()

        @pl.when(hi2 & lo2)
        def _():
            copy(4, c, buf_ref.at[1], down).start()

        @pl.when(hi2 & (odd == 0))
        def _():
            copy(5, c, buf_ref.at[1], across).start()

    level = lax.broadcasted_iota(jnp.int32, (qs_ref.shape[0], 1), 0)
    gain = jnp.sum(
        jnp.where(level == level_ref[0], qs_ref[...], 0.0), axis=0, keepdims=True
    )
    gain_ref[...] = gain
    queries = mm(x_ref[...], sp_ref[...]).astype(BF)
    q_ref[...] = queries
    qt_ref[...] = queries.T
    grad_z = ct_ref[...].astype(F32) * gain
    grad_zb = grad_z.astype(BF)
    gzb_ref[...] = grad_zb
    ct_copy.wait()
    outer = (cth_ref[...].astype(F32) * gain).astype(BF)
    blank = jnp.zeros_like(outer)
    ext_ref[COLS : COLS + tokens, :] = grad_zb

    @pl.when(r == 0)
    def _():
        ext_ref[:COLS, :] = blank
        ext_ref[COLS + tokens :, :] = outer

    @pl.when(r != 0)
    def _():
        ext_ref[:COLS, :] = outer
        ext_ref[COLS + tokens :, :] = blank

    resid = grad_z
    for t in range(3):
        resid = resid + mm(ext_ref[(2 - t) * COLS : (2 - t) * COLS + tokens, :], taps_ref[t], 1, 1)
    resid_ref[...] = resid
    grad_mixed = mm(resid.astype(BF), op_ref[...], 1, 1).astype(BF)
    do_ref[...] = grad_mixed
    dot_ref[...] = grad_mixed.T

    rim = WMAX * COLS
    start = pl.multiple_of((1 - r) * (tokens - rim), rim)

    def halo(kind):
        return pltpu.make_async_remote_copy(
            buf_ref.at[kind, pl.ds(start, rim)], halo_ref.at[kind], hs.at[kind], hr.at[kind],
            device_id=partner, device_id_type=MESH,
        )

    for kind in range(6):

        @pl.when(have[kind])
        def _():
            if kind > 1:
                for c in range(CHUNKS):
                    copy(kind, c, x_ref, across).wait_recv()
            halo(kind).start()

    sent = (hi2, lo2, always, lo2 & hi2, lo2 & hi2, (lo2 & (odd == 1)) | (hi2 & (odd == 0)))
    for kind in range(6):

        @pl.when(have[kind])
        def _():
            halo(kind).wait()

        @pl.when(sent[kind])
        def _():
            for c in range(CHUNKS):
                copy(kind, c, x_ref, across).wait_send()


def fetch(level, tokens, cotangent, scale, shared, output, taps, frames):
    count, width = tokens.shape
    vm = pl.BlockSpec(memory_space=pltpu.VMEM)
    dma = pltpu.SemaphoreType.DMA
    rows = jax.ShapeDtypeStruct((count, width), BF)
    columns = jax.ShapeDtypeStruct((width, count), BF)
    return pl.pallas_call(
        functools.partial(fetch_kernel, frames),
        out_shape=(
            jax.ShapeDtypeStruct((6, count, width), BF),
            jax.ShapeDtypeStruct((6, WMAX * COLS, width), BF),
            rows, columns, rows, columns, rows,
            jax.ShapeDtypeStruct((count, width), F32),
            jax.ShapeDtypeStruct((1, width), F32),
        ),
        in_specs=[pl.BlockSpec(memory_space=pltpu.SMEM)] + [vm] * 6,
        out_specs=(vm,) * 9,
        scratch_shapes=[
            pltpu.VMEM((COLS, width), BF),
            pltpu.VMEM((count + 2 * COLS, width), BF),
            dma((6, CHUNKS)), dma((6, CHUNKS)), dma((6,)), dma((6,)), dma(()), dma(()),
        ],
        compiler_params=pltpu.CompilerParams(collective_id=0, has_side_effects=True),
        name="fetch",
    )(level, tokens, cotangent, scale, shared, output, taps)


def reduce_kernel(
    frames, out_ref, base_ref, w_ref, lat_ref, wsum_ref,
    rb, sb, wp, ws, wr, ssem, rsem, ps, pr, rs_s, rs_r, ag_s, ag_r, fw_s, fw_r,
):
    f = lax.axis_index("frame")
    r = lax.axis_index("row")
    tokens = base_ref.shape[0]
    odd = lax.rem(f, 2)
    pair = f + 1 - 2 * odd
    lo2, hi2, lo4, hi4 = f >= 2, f + 2 < frames, f >= 4, f + 4 < frames
    always = f >= 0
    side = ((odd == 1) & (f + 1 < frames)) | ((odd == 0) & (f >= 1))
    relay = ((odd == 1) & lo2) | ((odd == 0) & hi2)
    partner = {"row": 1 - r}
    up, down, across = {"frame": f + 2}, {"frame": f - 2}, {"frame": pair}

    barrier = pltpu.get_barrier_semaphore()
    pl.semaphore_signal(barrier, inc=1, device_id=partner, device_id_type=MESH)

    def hello(k, carry):
        pl.semaphore_signal(
            barrier, inc=1, device_id={"frame": lax.rem(f + k, frames)}, device_id_type=MESH
        )
        return carry

    lax.fori_loop(1, frames, hello, 0)
    pl.semaphore_wait(barrier, frames)

    step = tokens // CHUNKS
    sent = (hi2, lo2, always, hi4, lo4, side)
    got = (lo2, hi2, always, lo2 & hi2, lo2 & hi2, relay)
    device = (up, down, across, up, down, across)

    def copy(kind, c, source):
        part = pl.ds(c * step, step)
        return pltpu.make_async_remote_copy(
            source.at[part], rb.at[kind, part], ssem.at[kind, c], rsem.at[kind, c],
            device_id=device[kind], device_id_type=MESH,
        )

    halves = pltpu.make_async_remote_copy(
        w_ref.at[1 - r], wp, ps, pr, device_id=partner, device_id_type=MESH
    )
    halves.start()
    for c in range(CHUNKS):
        for kind in (3, 4, 5):

            @pl.when(sent[kind])
            def _():
                copy(kind, c, out_ref.at[kind]).start()

    for kind in (0, 1, 3, 4, 5):

        @pl.when(jnp.logical_not(got[kind]))
        def _():
            rb[kind, :, :] = jnp.zeros((tokens, rb.shape[2]), BF)

    halves.wait()
    ws[...] = (w_ref[r] + wp[...]).astype(BF)

    def piece(ref, mine, other, target, s_sem, r_sem, slot, k):
        return pltpu.make_async_remote_copy(
            mine, other, s_sem.at[k], r_sem.at[slot],
            device_id={"frame": target}, device_id_type=MESH,
        )

    def scatter(k):
        target = lax.rem(f + k, frames)
        return piece(ws, ws.at[target], wr.at[f], target, rs_s, rs_r, f, k)

    def arrived(k):
        source = lax.rem(f - k + frames, frames)
        return source, piece(ws, ws.at[source], wr.at[source], source, rs_s, rs_r, source, k)

    def gather(k):
        target = lax.rem(f + k, frames)
        return piece(ws, wsum_ref.at[r, f], wsum_ref.at[r, f], target, ag_s, ag_r, f, k)

    def gathered(k):
        source = lax.rem(f - k + frames, frames)
        return source, piece(
            ws, wsum_ref.at[r, source], wsum_ref.at[r, source], source, ag_s, ag_r, source, k
        )

    def forward(j, own):
        return pltpu.make_async_remote_copy(
            wsum_ref.at[own, j], wsum_ref.at[own, j], fw_s.at[j], fw_r.at[j],
            device_id=partner, device_id_type=MESH,
        )

    def run(body):
        lax.fori_loop(1, frames, lambda k, carry: (body(k), carry)[1], 0)

    run(lambda k: scatter(k).start())
    for c in range(CHUNKS):
        copy(2, c, out_ref.at[2]).start()

    even = jnp.where(odd == 0, 1.0, 0.0).astype(F32)
    for c in range(CHUNKS):
        part = slice(c * step, (c + 1) * step)
        for kind in (3, 4, 5):

            @pl.when(got[kind])
            def _():
                copy(kind, c, out_ref.at[kind]).wait_recv()

        extra = rb[5, part, :].astype(F32)
        rising = out_ref[0, part, :].astype(F32) + rb[3, part, :].astype(F32) + extra * even
        falling = (
            out_ref[1, part, :].astype(F32) + rb[4, part, :].astype(F32) + extra * (1.0 - even)
        )
        sb[0, part, :] = rising.astype(BF)
        sb[1, part, :] = falling.astype(BF)

        @pl.when(hi2)
        def _():
            copy(0, c, sb.at[0]).start()

        @pl.when(lo2)
        def _():
            copy(1, c, sb.at[1]).start()

    def add_piece(k, total):
        source, waiting = arrived(k)
        waiting.wait_recv()
        return total + wr[source].astype(F32)

    total = lax.fori_loop(1, frames, add_piece, w_ref[r, f] + wp[f])
    wsum_ref[r, f] = total.astype(BF)
    run(lambda k: gather(k).start())
    forward(f, r).start()

    for c in range(CHUNKS):
        part = slice(c * step, (c + 1) * step)
        for kind in (0, 1, 2):

            @pl.when(got[kind])
            def _():
                copy(kind, c, out_ref.at[kind]).wait_recv()

        lat_ref[part, :] = (
            base_ref[part, :]
            + rb[0, part, :].astype(F32)
            + rb[1, part, :].astype(F32)
            + rb[2, part, :].astype(F32)
        ).astype(BF)

    def pass_on(k):
        source, waiting = gathered(k)
        waiting.wait_recv()
        forward(source, r).start()

    run(pass_on)

    def finish(k):
        scatter(k).wait_send()
        gather(k).wait_send()

    run(finish)

    def last(j, carry):
        forward(j, r).wait_send()
        forward(j, 1 - r).wait_recv()
        return carry

    lax.fori_loop(0, frames, last, 0)
    for kind in range(6):

        @pl.when(sent[kind])
        def _():
            for c in range(CHUNKS):
                copy(kind, c, out_ref.at[kind]).wait_send()


def reduce(outgoing, base, grads, frames):
    count, width = base.shape
    vm = pl.BlockSpec(memory_space=pltpu.VMEM)
    dma = pltpu.SemaphoreType.DMA
    pieces = grads.shape[1:]
    return pl.pallas_call(
        functools.partial(reduce_kernel, frames),
        out_shape=(
            jax.ShapeDtypeStruct((count, width), BF),
            jax.ShapeDtypeStruct(grads.shape, BF),
        ),
        in_specs=[vm] * 3,
        out_specs=(vm,) * 2,
        scratch_shapes=[
            pltpu.VMEM((6, count, width), BF),
            pltpu.VMEM((2, count, width), BF),
            pltpu.VMEM(pieces, F32),
            pltpu.VMEM(pieces, BF),
            pltpu.VMEM(pieces, BF),
            dma((6, CHUNKS)), dma((6, CHUNKS)), dma(()), dma(()),
            dma((frames,)), dma((frames,)), dma((frames,)), dma((frames,)),
            dma((frames,)), dma((frames,)),
        ],
        compiler_params=pltpu.CompilerParams(collective_id=1, has_side_effects=True),
        name="reduce",
    )(outgoing, base, grads)


def from_partner(value):
    return lax.ppermute(value, "row", [(0, 1), (1, 0)])


def row_halo(array, row_id, width):
    length = array.shape[-3]
    first = lax.slice_in_dim(array, 0, width, axis=array.ndim - 3)
    last = lax.slice_in_dim(array, length - width, length, axis=array.ndim - 3)
    got = from_partner(jnp.where(row_id == 0, last, first))
    zero = jnp.zeros_like(got)
    before = jnp.where(row_id == 0, zero, got)
    after = jnp.where(row_id == 0, got, zero)
    return jnp.concatenate([before, array, after], axis=array.ndim - 3)


def local(
    latents, ref_frames, windows, quant_level, quant_scale,
    shared_proj, value_proj, output_proj, conv_taps, cotangent,
):
    width = latents.shape[2]
    rows_dev = latents.shape[1] // COLS
    row_devs = lax.axis_size("row")
    total_rows = rows_dev * row_devs
    frame_id = lax.axis_index("frame")
    row_id = lax.axis_index("row")
    own_refs = ref_frames[0]
    ext_rows = rows_dev + 2 * WMAX
    grid = (rows_dev, COLS, width)
    tokens = latents[0]
    frames = lax.axis_size("frame")
    odd = frame_id % 2
    sources = (
        frame_id - 2, frame_id + 2, frame_id + 1 - 2 * odd,
        frame_id - 4, frame_id + 4, frame_id - 1 + 2 * odd,
    )
    buf, halo, q, qt, do, dot, grad_zb, grad_resid, gain = fetch(
        quant_level, tokens, cotangent[0], quant_scale, shared_proj, output_proj, conv_taps, frames
    )
    kinds = jnp.zeros((2,), jnp.int32)
    for kind, source in enumerate(sources):
        kinds = jnp.where(own_refs == source, kind, kinds)
    rest = jnp.stack([windows[0], row_id, jnp.int32(total_rows)]).astype(jnp.int32)
    meta = jnp.concatenate([kinds, rest])
    residual, hidden, grad_latents, partial, grad_shared, grad_values, grad_output = attention(
        meta, buf, halo, tokens, q, qt, do, dot, grad_resid, shared_proj, value_proj, output_proj
    )
    hidden_ext = row_halo(hidden.reshape(grid), row_id, 1).reshape(-1, width)
    context = residual
    for t in range(3):
        context = context + mm(hidden_ext[t * COLS : (t + rows_dev) * COLS], conv_taps[t])
    coded = (context * gain).astype(BF)

    partial = partial.reshape(2, ext_rows, COLS, width)
    upper = partial[:, :WMAX]
    lower = partial[:, WMAX + rows_dev :]
    got = from_partner(jnp.where(row_id == 0, lower, upper).astype(BF)).astype(F32)
    filler = jnp.zeros((2, rows_dev - WMAX, COLS, width), F32)
    middle = (
        partial[:, WMAX : WMAX + rows_dev]
        + jnp.concatenate([jnp.where(row_id == 0, 0.0, got), filler], axis=1)
        + jnp.concatenate([filler, jnp.where(row_id == 0, got, 0.0)], axis=1)
    )
    targets = (
        frame_id + 2, frame_id - 2, frame_id + 1 - 2 * odd,
        frame_id + 4, frame_id - 4, frame_id - 1 + 2 * odd,
    )
    outgoing = jnp.stack(
        [
            jnp.sum(jnp.where((own_refs == t).reshape(2, 1, 1, 1), middle, 0.0), axis=0)
            .astype(BF)
            .reshape(-1, width)
            for t in targets
        ]
    )
    grad_taps = jnp.stack(
        [mm(hidden_ext[t * COLS : (t + rows_dev) * COLS], grad_zb, 0, 0) for t in range(3)]
    )
    stacked = jnp.concatenate(
        [grad_shared, grad_values, grad_output, grad_taps.reshape(-1, width)], axis=0
    )
    grads = stacked.reshape(2, frames, stacked.shape[0] // (2 * frames), width)
    new_latents, summed = reduce(outgoing, grad_latents, grads, frames)
    norm = 1.0 / math.sqrt(frames * total_rows * COLS)
    summed = summed.reshape(-1, width).astype(F32) * norm
    return (
        coded[None],
        new_latents[None],
        summed[:width],
        summed[width : 2 * width],
        summed[2 * width : 3 * width],
        summed[3 * width :].reshape(3, width, width),
    )


def solution(mesh):
    tok = P(("groups", "frame"), "row", None)
    frm = P(("groups", "frame"))
    placed = (tok, P(("groups", "frame"), None), frm, frm, P(), P(), P(), P(), P(), tok)
    return jax.shard_map(
        local,
        mesh=mesh,
        in_specs=placed,
        out_specs=(
            tok, tok, P("groups", None), P("groups", None), P("groups", None),
            P("groups", None, None),
        ),
        check_vma=False,
    )
```

```python
import functools
import math

import jax
import jax.numpy as jnp
from jax import lax
from jax.experimental import pallas as pl
from jax.experimental.pallas import tpu as pltpu
from jax.sharding import PartitionSpec as P

HEADS = 8
DH = 32
COLS = 64
QBLK = 4
WMAX = 2

SCORE_SCALE = 1.5 / math.sqrt(DH)
LOG2E = math.log2(math.e)
BF = jnp.bfloat16
F32 = jnp.float32


def mm(a, b, ca=1, cb=0):
    return lax.dot_general(a, b, (((ca,), (cb,)), ((), ())), preferred_element_type=F32)


def attention_kernel(
    meta_ref, buf_hbm, halo_hbm, x_hbm, q_hbm, qt_hbm, do_hbm, dot_hbm, resid_hbm,
    sp_ref, vp_ref, op_ref,
    residual_ref, hidden_ref, base_ref, part_ref, gs_ref, gv_ref, go_ref,
    xs_ref, k_ref, v_ref, kt_ref, vt_ref, mixt_ref, dqt_ref, dk_ref, dv_ref,
    s_scr, dp_scr, p_scr, ds_scr, qm_scr, dom_scr,
    x_ref, q_ref, qt_ref, do_ref, dot_ref, resid_ref, sems,
):
    tokens, width = q_ref.shape
    nq = QBLK * COLS
    span = (QBLK + 2 * WMAX) * COLS
    rows = span // COLS
    blocks = tokens // nq
    half = width // 2
    per_half = HEADS // 2
    lane = lax.broadcasted_iota(jnp.int32, (1, width), 1) // DH
    sub = lax.broadcasted_iota(jnp.int32, (half, 1), 0) // DH

    dk_ref[...] = jnp.zeros_like(dk_ref)
    dv_ref[...] = jnp.zeros_like(dv_ref)
    rim = WMAX * COLS
    window = meta_ref[2]
    row_id = meta_ref[3]
    first_row = row_id * (tokens // COLS)
    total_rows = meta_ref[4]
    bottom = rim + tokens
    held = pl.multiple_of(jnp.where(row_id == 0, bottom, 0), rim)
    empty = pl.multiple_of(jnp.where(row_id == 0, 0, bottom), rim)
    moves = []
    for s in range(2):
        kind = meta_ref[s]
        moves.append((buf_hbm.at[kind], xs_ref.at[s, pl.ds(rim, tokens)]))
        moves.append((halo_hbm.at[kind], xs_ref.at[s, pl.ds(held, rim)]))
    moves += [
        (q_hbm, q_ref), (do_hbm, do_ref), (qt_hbm, qt_ref), (dot_hbm, dot_ref),
        (x_hbm, x_ref), (resid_hbm, resid_ref),
    ]
    copies = [
        pltpu.make_async_copy(source, target, sems.at[i])
        for i, (source, target) in enumerate(moves)
    ]
    for move in copies:
        move.start()
    for s in range(2):
        xs_ref[s, pl.ds(empty, rim), :] = jnp.zeros((rim, width), BF)
        copies[2 * s].wait()
        copies[2 * s + 1].wait()
        xs = xs_ref[s]
        keys = mm(xs, sp_ref[...]).astype(BF)
        vals = mm(xs, vp_ref[...]).astype(BF)
        k_ref[s] = keys
        v_ref[s] = vals
        kt_ref[s] = keys.T
        vt_ref[s] = vals.T
    for move in copies[4:]:
        move.wait()
    query_row = lax.broadcasted_iota(jnp.int32, (1, nq), 1) // COLS

    def bias_row(b, c):
        key_row = first_row + b * QBLK + c - WMAX
        reach = jnp.where((key_row >= 0) & (key_row < total_rows), window, -1)
        return jnp.where(jnp.abs(c - WMAX - query_row) <= reach, 0.0, -jnp.inf).astype(F32)

    for b in range(blocks):
        q0 = b * nq
        qb = q_ref[q0 : q0 + nq, :]
        dob = do_ref[q0 : q0 + nq, :]
        for h in range(HEADS):
            keep = lane == h
            qm_scr[h * nq : (h + 1) * nq, :] = jnp.where(keep, qb, jnp.zeros_like(qb))
            dom_scr[h * nq : (h + 1) * nq, :] = jnp.where(keep, dob, jnp.zeros_like(dob))

        for hf in range(2):
            f0 = hf * half
            qth = qt_ref[f0 : f0 + half, q0 : q0 + nq]
            doth = dot_ref[f0 : f0 + half, q0 : q0 + nq]

            def one_head(hh, carry, hf=hf, f0=f0, qth=qth, doth=doth, q0=q0, b=b):
                keep = sub == hh
                qtm = jnp.where(keep, qth, jnp.zeros_like(qth))
                dotm = jnp.where(keep, doth, jnp.zeros_like(doth))
                for s in range(2):
                    s_scr[s * span : (s + 1) * span, :] = mm(
                        k_ref[s, q0 : q0 + span, f0 : f0 + half], qtm
                    )
                    dp_scr[s * span : (s + 1) * span, :] = mm(
                        v_ref[s, q0 : q0 + span, f0 : f0 + half], dotm
                    )
                m8 = jnp.full((8, nq), -jnp.inf, F32)
                for c in range(2 * rows):
                    x = s_scr[c * COLS : (c + 1) * COLS, :].reshape(COLS // 8, 8, nq)
                    m8 = jnp.maximum(m8, jnp.max(x, axis=0) + bias_row(b, c % rows))
                m = jnp.max(m8, axis=0, keepdims=True)
                kk = SCORE_SCALE * LOG2E
                l8 = jnp.zeros((8, nq), F32)
                u8 = jnp.zeros((8, nq), F32)
                for c in range(2 * rows):
                    sl = slice(c * COLS, (c + 1) * COLS)
                    off = (bias_row(b, c % rows) - m) * kk
                    p = jnp.exp2(s_scr[sl, :] * kk + off)
                    s_scr[sl, :] = p
                    l8 = l8 + jnp.sum(p.reshape(COLS // 8, 8, nq), axis=0)
                    u8 = u8 + jnp.sum((p * dp_scr[sl, :]).reshape(COLS // 8, 8, nq), axis=0)
                inv = 1.0 / jnp.sum(l8, axis=0, keepdims=True)
                ci = inv * SCORE_SCALE
                inner = jnp.sum(u8, axis=0, keepdims=True) * inv * ci
                col = pl.multiple_of((hf * per_half + hh) * nq, nq)
                for c in range(2 * rows):
                    sl = slice(c * COLS, (c + 1) * COLS)
                    p = s_scr[sl, :]
                    p_scr[sl, pl.ds(col, nq)] = (p * inv).astype(BF)
                    ds_scr[sl, pl.ds(col, nq)] = (p * (dp_scr[sl, :] * ci - inner)).astype(BF)
                r0 = pl.multiple_of(f0 + hh * DH, DH)
                mix = jnp.zeros((DH, nq), F32)
                dq = jnp.zeros((DH, nq), F32)
                for s in range(2):
                    ks = slice(s * span, (s + 1) * span)
                    mix = mix + mm(
                        vt_ref[s, pl.ds(r0, DH), q0 : q0 + span], p_scr[ks, pl.ds(col, nq)]
                    )
                    dq = dq + mm(
                        kt_ref[s, pl.ds(r0, DH), q0 : q0 + span], ds_scr[ks, pl.ds(col, nq)]
                    )
                mixt_ref[pl.ds(r0, DH), q0 : q0 + nq] = mix.astype(BF)
                dqt_ref[pl.ds(r0, DH), q0 : q0 + nq] = dq
                return carry

            lax.fori_loop(0, per_half, one_head, 0)

        for s in range(2):
            ks = slice(s * span, (s + 1) * span)
            dk_ref[s, q0 : q0 + span, :] += mm(ds_scr[ks, :], qm_scr[...])
            dv_ref[s, q0 : q0 + span, :] += mm(p_scr[ks, :], dom_scr[...])

    dq = dqt_ref[...].T.astype(BF)
    base_ref[...] = resid_ref[...] + mm(dq, sp_ref[...], 1, 1)
    mixt = mixt_ref[...]
    go_ref[...] = mm(mixt, resid_ref[...].astype(BF))
    residual = x_ref[...].astype(F32) + mm(mixt.T, op_ref[...])
    residual_ref[...] = residual
    hidden_ref[...] = residual.astype(BF)
    gs = mm(x_ref[...].T, dq)
    gv = jnp.zeros((width, width), F32)
    for s in range(2):
        dk = dk_ref[s].astype(BF)
        dv = dv_ref[s].astype(BF)
        part_ref[s] = mm(dk, sp_ref[...], 1, 1) + mm(dv, vp_ref[...], 1, 1)
        xst = xs_ref[s].T
        gs = gs + mm(xst, dk)
        gv = gv + mm(xst, dv)
    gs_ref[...] = gs
    gv_ref[...] = gv


def attention(meta, buf, halo, x, q, qt, do, dot, resid, shared, value, output):
    tokens, width = q.shape
    ext = tokens + 2 * WMAX * COLS
    nq = QBLK * COLS
    keys = 2 * (QBLK + 2 * WMAX) * COLS
    vm = pl.BlockSpec(memory_space=pltpu.VMEM)
    full = jax.ShapeDtypeStruct((tokens, width), F32)
    square = jax.ShapeDtypeStruct((width, width), F32)
    return pl.pallas_call(
        attention_kernel,
        out_shape=(
            full,
            jax.ShapeDtypeStruct((tokens, width), BF),
            full,
            jax.ShapeDtypeStruct((2, ext, width), F32),
            square, square, square,
        ),
        in_specs=[pl.BlockSpec(memory_space=pltpu.SMEM)]
        + [pl.BlockSpec(memory_space=pltpu.MemorySpace.HBM)] * 8
        + [vm] * 3,
        out_specs=(vm,) * 7,
        scratch_shapes=[
            pltpu.VMEM((2, ext, width), BF),
            pltpu.VMEM((2, ext, width), BF),
            pltpu.VMEM((2, ext, width), BF),
            pltpu.VMEM((2, width, ext), BF),
            pltpu.VMEM((2, width, ext), BF),
            pltpu.VMEM((width, tokens), BF),
            pltpu.VMEM((width, tokens), F32),
            pltpu.VMEM((2, ext, width), F32),
            pltpu.VMEM((2, ext, width), F32),
            pltpu.VMEM((keys, nq), F32),
            pltpu.VMEM((keys, nq), F32),
            pltpu.VMEM((keys, HEADS * nq), BF),
            pltpu.VMEM((keys, HEADS * nq), BF),
            pltpu.VMEM((HEADS * nq, width), BF),
            pltpu.VMEM((HEADS * nq, width), BF),
            pltpu.VMEM((tokens, width), BF),
            pltpu.VMEM((tokens, width), BF),
            pltpu.VMEM((width, tokens), BF),
            pltpu.VMEM((tokens, width), BF),
            pltpu.VMEM((width, tokens), BF),
            pltpu.VMEM((tokens, width), F32),
            pltpu.SemaphoreType.DMA((10,)),
        ],
        compiler_params=pltpu.CompilerParams(vmem_limit_bytes=66_000_000),
        cost_estimate=pl.CostEstimate(
            flops=int(2e10), bytes_accessed=int(8e6), transcendentals=int(4e6)
        ),
        name="attention",
    )(meta, buf, halo, x, q, qt, do, dot, resid, shared, value, output)


MESH = pl.DeviceIdType.MESH
CHUNKS = 4


def greet(targets):
    barrier = pltpu.get_barrier_semaphore()
    count = 0
    for exists, device in targets:

        @pl.when(exists)
        def _(device=device):
            pl.semaphore_signal(barrier, inc=1, device_id=device, device_id_type=MESH)

        count = count + jnp.where(exists, 1, 0)
    pl.semaphore_wait(barrier, count)


def fetch_kernel(
    frames, level_ref, x_ref, ct_ref, qs_ref, sp_ref, op_ref, taps_ref,
    buf_ref, halo_ref, q_ref, qt_ref, do_ref, dot_ref, gzb_ref, resid_ref, gain_ref,
    cth_ref, ext_ref, ssem, rsem, hs, hr, cs, cr,
):
    f = lax.axis_index("frame")
    r = lax.axis_index("row")
    tokens = x_ref.shape[0]
    odd = lax.rem(f, 2)
    pair = f + 1 - 2 * odd
    lo2, hi2, lo4, hi4 = f >= 2, f + 2 < frames, f >= 4, f + 4 < frames
    side = ((odd == 1) & (f + 1 < frames)) | ((odd == 0) & (f >= 1))
    always = f >= 0
    have = (lo2, hi2, always, lo4, hi4, side)
    partner = {"row": 1 - r}
    up, down, across = {"frame": f + 2}, {"frame": f - 2}, {"frame": pair}
    greet(((hi2, up), (lo2, down), (always, across), (always, partner)))

    edge = ct_ref.shape[0] - COLS
    ct_copy = pltpu.make_async_remote_copy(
        ct_ref.at[pl.ds(pl.multiple_of((1 - r) * edge, COLS), COLS)], cth_ref, cs, cr,
        device_id=partner, device_id_type=MESH,
    )
    ct_copy.start()
    step = tokens // CHUNKS

    def copy(kind, c, source, device):
        part = pl.ds(c * step, step)
        return pltpu.make_async_remote_copy(
            source.at[part], buf_ref.at[kind, part], ssem.at[kind, c], rsem.at[kind, c],
            device_id=device, device_id_type=MESH,
        )

    for c in range(CHUNKS):

        @pl.when(hi2)
        def _():
            copy(0, c, x_ref, up).start()

        @pl.when(lo2)
        def _():
            copy(1, c, x_ref, down).start()

        copy(2, c, x_ref, across).start()

    for c in range(CHUNKS):

        @pl.when(lo2)
        def _():
            copy(0, c, x_ref, across).wait_recv()

        @pl.when(lo2 & hi2)
        def _():
            copy(3, c, buf_ref.at[0], up).start()

        @pl.when(lo2 & (odd == 1))
        def _():
            copy(5, c, buf_ref.at[0], across).start()

        @pl.when(hi2)
        def _():
            copy(1, c, x_ref, across).wait_recv()

        @pl.when(hi2 & lo2)
        def _():
            copy(4, c, buf_ref.at[1], down).start()

        @pl.when(hi2 & (odd == 0))
        def _():
            copy(5, c, buf_ref.at[1], across).start()

    level = lax.broadcasted_iota(jnp.int32, (qs_ref.shape[0], 1), 0)
    gain = jnp.sum(
        jnp.where(level == level_ref[0], qs_ref[...], 0.0), axis=0, keepdims=True
    )
    gain_ref[...] = gain
    queries = mm(x_ref[...], sp_ref[...]).astype(BF)
    q_ref[...] = queries
    qt_ref[...] = queries.T
    grad_z = ct_ref[...].astype(F32) * gain
    grad_zb = grad_z.astype(BF)
    gzb_ref[...] = grad_zb
    ct_copy.wait()
    outer = (cth_ref[...].astype(F32) * gain).astype(BF)
    blank = jnp.zeros_like(outer)
    ext_ref[COLS : COLS + tokens, :] = grad_zb

    @pl.when(r == 0)
    def _():
        ext_ref[:COLS, :] = blank
        ext_ref[COLS + tokens :, :] = outer

    @pl.when(r != 0)
    def _():
        ext_ref[:COLS, :] = outer
        ext_ref[COLS + tokens :, :] = blank

    resid = grad_z
    for t in range(3):
        resid = resid + mm(ext_ref[(2 - t) * COLS : (2 - t) * COLS + tokens, :], taps_ref[t], 1, 1)
    resid_ref[...] = resid
    grad_mixed = mm(resid.astype(BF), op_ref[...], 1, 1).astype(BF)
    do_ref[...] = grad_mixed
    dot_ref[...] = grad_mixed.T

    rim = WMAX * COLS
    start = pl.multiple_of((1 - r) * (tokens - rim), rim)

    def halo(kind):
        return pltpu.make_async_remote_copy(
            buf_ref.at[kind, pl.ds(start, rim)], halo_ref.at[kind], hs.at[kind], hr.at[kind],
            device_id=partner, device_id_type=MESH,
        )

    for kind in range(6):

        @pl.when(have[kind])
        def _():
            if kind > 1:
                for c in range(CHUNKS):
                    copy(kind, c, x_ref, across).wait_recv()
            halo(kind).start()

    sent = (hi2, lo2, always, lo2 & hi2, lo2 & hi2, (lo2 & (odd == 1)) | (hi2 & (odd == 0)))
    for kind in range(6):

        @pl.when(have[kind])
        def _():
            halo(kind).wait()

        @pl.when(sent[kind])
        def _():
            for c in range(CHUNKS):
                copy(kind, c, x_ref, across).wait_send()


def fetch(level, tokens, cotangent, scale, shared, output, taps, frames):
    count, width = tokens.shape
    vm = pl.BlockSpec(memory_space=pltpu.VMEM)
    dma = pltpu.SemaphoreType.DMA
    rows = jax.ShapeDtypeStruct((count, width), BF)
    columns = jax.ShapeDtypeStruct((width, count), BF)
    return pl.pallas_call(
        functools.partial(fetch_kernel, frames),
        out_shape=(
            jax.ShapeDtypeStruct((6, count, width), BF),
            jax.ShapeDtypeStruct((6, WMAX * COLS, width), BF),
            rows, columns, rows, columns, rows,
            jax.ShapeDtypeStruct((count, width), F32),
            jax.ShapeDtypeStruct((1, width), F32),
        ),
        in_specs=[pl.BlockSpec(memory_space=pltpu.SMEM)] + [vm] * 6,
        out_specs=(vm,) * 9,
        scratch_shapes=[
            pltpu.VMEM((COLS, width), BF),
            pltpu.VMEM((count + 2 * COLS, width), BF),
            dma((6, CHUNKS)), dma((6, CHUNKS)), dma((6,)), dma((6,)), dma(()), dma(()),
        ],
        compiler_params=pltpu.CompilerParams(collective_id=0, has_side_effects=True),
        name="fetch",
    )(level, tokens, cotangent, scale, shared, output, taps)


def reduce_kernel(
    frames, out_ref, base_ref, w_ref, lat_ref, wsum_ref,
    rb, sb, wp, ws, wr, ssem, rsem, ps, pr, rs_s, rs_r, ag_s, ag_r, fw_s, fw_r,
):
    f = lax.axis_index("frame")
    r = lax.axis_index("row")
    tokens = base_ref.shape[0]
    odd = lax.rem(f, 2)
    pair = f + 1 - 2 * odd
    lo2, hi2, lo4, hi4 = f >= 2, f + 2 < frames, f >= 4, f + 4 < frames
    always = f >= 0
    side = ((odd == 1) & (f + 1 < frames)) | ((odd == 0) & (f >= 1))
    relay = ((odd == 1) & lo2) | ((odd == 0) & hi2)
    partner = {"row": 1 - r}
    up, down, across = {"frame": f + 2}, {"frame": f - 2}, {"frame": pair}

    barrier = pltpu.get_barrier_semaphore()
    pl.semaphore_signal(barrier, inc=1, device_id=partner, device_id_type=MESH)

    def hello(k, carry):
        pl.semaphore_signal(
            barrier, inc=1, device_id={"frame": lax.rem(f + k, frames)}, device_id_type=MESH
        )
        return carry

    lax.fori_loop(1, frames, hello, 0)
    pl.semaphore_wait(barrier, frames)

    step = tokens // CHUNKS
    sent = (hi2, lo2, always, hi4, lo4, side)
    got = (lo2, hi2, always, lo2 & hi2, lo2 & hi2, relay)
    device = (up, down, across, up, down, across)

    def copy(kind, c, source):
        part = pl.ds(c * step, step)
        return pltpu.make_async_remote_copy(
            source.at[part], rb.at[kind, part], ssem.at[kind, c], rsem.at[kind, c],
            device_id=device[kind], device_id_type=MESH,
        )

    halves = pltpu.make_async_remote_copy(
        w_ref.at[1 - r], wp, ps, pr, device_id=partner, device_id_type=MESH
    )
    halves.start()
    for c in range(CHUNKS):
        for kind in (3, 4, 5):

            @pl.when(sent[kind])
            def _():
                copy(kind, c, out_ref.at[kind]).start()

    for kind in (0, 1, 3, 4, 5):

        @pl.when(jnp.logical_not(got[kind]))
        def _():
            rb[kind, :, :] = jnp.zeros((tokens, rb.shape[2]), BF)

    halves.wait()
    ws[...] = (w_ref[r] + wp[...]).astype(BF)

    def piece(ref, mine, other, target, s_sem, r_sem, slot, k):
        return pltpu.make_async_remote_copy(
            mine, other, s_sem.at[k], r_sem.at[slot],
            device_id={"frame": target}, device_id_type=MESH,
        )

    def scatter(k):
        target = lax.rem(f + k, frames)
        return piece(ws, ws.at[target], wr.at[f], target, rs_s, rs_r, f, k)

    def arrived(k):
        source = lax.rem(f - k + frames, frames)
        return source, piece(ws, ws.at[source], wr.at[source], source, rs_s, rs_r, source, k)

    def gather(k):
        target = lax.rem(f + k, frames)
        return piece(ws, wsum_ref.at[r, f], wsum_ref.at[r, f], target, ag_s, ag_r, f, k)

    def gathered(k):
        source = lax.rem(f - k + frames, frames)
        return source, piece(
            ws, wsum_ref.at[r, source], wsum_ref.at[r, source], source, ag_s, ag_r, source, k
        )

    def forward(j, own):
        return pltpu.make_async_remote_copy(
            wsum_ref.at[own, j], wsum_ref.at[own, j], fw_s.at[j], fw_r.at[j],
            device_id=partner, device_id_type=MESH,
        )

    def run(body):
        lax.fori_loop(1, frames, lambda k, carry: (body(k), carry)[1], 0)

    run(lambda k: scatter(k).start())
    for c in range(CHUNKS):
        copy(2, c, out_ref.at[2]).start()

    even = jnp.where(odd == 0, 1.0, 0.0).astype(F32)
    for c in range(CHUNKS):
        part = slice(c * step, (c + 1) * step)
        for kind in (3, 4, 5):

            @pl.when(got[kind])
            def _():
                copy(kind, c, out_ref.at[kind]).wait_recv()

        extra = rb[5, part, :].astype(F32)
        rising = out_ref[0, part, :].astype(F32) + rb[3, part, :].astype(F32) + extra * even
        falling = (
            out_ref[1, part, :].astype(F32) + rb[4, part, :].astype(F32) + extra * (1.0 - even)
        )
        sb[0, part, :] = rising.astype(BF)
        sb[1, part, :] = falling.astype(BF)

        @pl.when(hi2)
        def _():
            copy(0, c, sb.at[0]).start()

        @pl.when(lo2)
        def _():
            copy(1, c, sb.at[1]).start()

    def add_piece(k, total):
        source, waiting = arrived(k)
        waiting.wait_recv()
        return total + wr[source].astype(F32)

    total = lax.fori_loop(1, frames, add_piece, w_ref[r, f] + wp[f])
    wsum_ref[r, f] = total.astype(BF)
    run(lambda k: gather(k).start())
    forward(f, r).start()

    for c in range(CHUNKS):
        part = slice(c * step, (c + 1) * step)
        for kind in (0, 1, 2):

            @pl.when(got[kind])
            def _():
                copy(kind, c, out_ref.at[kind]).wait_recv()

        lat_ref[part, :] = (
            base_ref[part, :]
            + rb[0, part, :].astype(F32)
            + rb[1, part, :].astype(F32)
            + rb[2, part, :].astype(F32)
        ).astype(BF)

    def pass_on(k):
        source, waiting = gathered(k)
        waiting.wait_recv()
        forward(source, r).start()

    run(pass_on)

    def finish(k):
        scatter(k).wait_send()
        gather(k).wait_send()

    run(finish)

    def last(j, carry):
        forward(j, r).wait_send()
        forward(j, 1 - r).wait_recv()
        return carry

    lax.fori_loop(0, frames, last, 0)
    for kind in range(6):

        @pl.when(sent[kind])
        def _():
            for c in range(CHUNKS):
                copy(kind, c, out_ref.at[kind]).wait_send()


def reduce(outgoing, base, grads, frames):
    count, width = base.shape
    vm = pl.BlockSpec(memory_space=pltpu.VMEM)
    dma = pltpu.SemaphoreType.DMA
    pieces = grads.shape[1:]
    return pl.pallas_call(
        functools.partial(reduce_kernel, frames),
        out_shape=(
            jax.ShapeDtypeStruct((count, width), BF),
            jax.ShapeDtypeStruct(grads.shape, BF),
        ),
        in_specs=[vm] * 3,
        out_specs=(vm,) * 2,
        scratch_shapes=[
            pltpu.VMEM((6, count, width), BF),
            pltpu.VMEM((2, count, width), BF),
            pltpu.VMEM(pieces, F32),
            pltpu.VMEM(pieces, BF),
            pltpu.VMEM(pieces, BF),
            dma((6, CHUNKS)), dma((6, CHUNKS)), dma(()), dma(()),
            dma((frames,)), dma((frames,)), dma((frames,)), dma((frames,)),
            dma((frames,)), dma((frames,)),
        ],
        compiler_params=pltpu.CompilerParams(collective_id=1, has_side_effects=True),
        name="reduce",
    )(outgoing, base, grads)


def from_partner(value):
    return lax.ppermute(value, "row", [(0, 1), (1, 0)])


def row_halo(array, row_id, width):
    length = array.shape[-3]
    first = lax.slice_in_dim(array, 0, width, axis=array.ndim - 3)
    last = lax.slice_in_dim(array, length - width, length, axis=array.ndim - 3)
    got = from_partner(jnp.where(row_id == 0, last, first))
    zero = jnp.zeros_like(got)
    before = jnp.where(row_id == 0, zero, got)
    after = jnp.where(row_id == 0, got, zero)
    return jnp.concatenate([before, array, after], axis=array.ndim - 3)


def local(
    latents, ref_frames, windows, quant_level, quant_scale,
    shared_proj, value_proj, output_proj, conv_taps, cotangent,
):
    width = latents.shape[2]
    rows_dev = latents.shape[1] // COLS
    row_devs = lax.axis_size("row")
    total_rows = rows_dev * row_devs
    frame_id = lax.axis_index("frame")
    row_id = lax.axis_index("row")
    own_refs = ref_frames[0]
    ext_rows = rows_dev + 2 * WMAX
    grid = (rows_dev, COLS, width)
    tokens = latents[0]
    frames = lax.axis_size("frame")
    odd = frame_id % 2
    sources = (
        frame_id - 2, frame_id + 2, frame_id + 1 - 2 * odd,
        frame_id - 4, frame_id + 4, frame_id - 1 + 2 * odd,
    )
    buf, halo, q, qt, do, dot, grad_zb, grad_resid, gain = fetch(
        quant_level, tokens, cotangent[0], quant_scale, shared_proj, output_proj, conv_taps, frames
    )
    kinds = jnp.zeros((2,), jnp.int32)
    for kind, source in enumerate(sources):
        kinds = jnp.where(own_refs == source, kind, kinds)
    rest = jnp.stack([windows[0], row_id, jnp.int32(total_rows)]).astype(jnp.int32)
    meta = jnp.concatenate([kinds, rest])
    residual, hidden, grad_latents, partial, grad_shared, grad_values, grad_output = attention(
        meta, buf, halo, tokens, q, qt, do, dot, grad_resid, shared_proj, value_proj, output_proj
    )
    hidden_ext = row_halo(hidden.reshape(grid), row_id, 1).reshape(-1, width)
    context = residual
    for t in range(3):
        context = context + mm(hidden_ext[t * COLS : (t + rows_dev) * COLS], conv_taps[t])
    coded = (context * gain).astype(BF)

    partial = partial.reshape(2, ext_rows, COLS, width)
    upper = partial[:, :WMAX]
    lower = partial[:, WMAX + rows_dev :]
    got = from_partner(jnp.where(row_id == 0, lower, upper).astype(BF)).astype(F32)
    filler = jnp.zeros((2, rows_dev - WMAX, COLS, width), F32)
    middle = (
        partial[:, WMAX : WMAX + rows_dev]
        + jnp.concatenate([jnp.where(row_id == 0, 0.0, got), filler], axis=1)
        + jnp.concatenate([filler, jnp.where(row_id == 0, got, 0.0)], axis=1)
    )
    targets = (
        frame_id + 2, frame_id - 2, frame_id + 1 - 2 * odd,
        frame_id + 4, frame_id - 4, frame_id - 1 + 2 * odd,
    )
    outgoing = jnp.stack(
        [
            jnp.sum(jnp.where((own_refs == t).reshape(2, 1, 1, 1), middle, 0.0), axis=0)
            .astype(BF)
            .reshape(-1, width)
            for t in targets
        ]
    )
    grad_taps = jnp.stack(
        [mm(hidden_ext[t * COLS : (t + rows_dev) * COLS], grad_zb, 0, 0) for t in range(3)]
    )
    stacked = jnp.concatenate(
        [grad_shared, grad_values, grad_output, grad_taps.reshape(-1, width)], axis=0
    )
    grads = stacked.reshape(2, frames, stacked.shape[0] // (2 * frames), width)
    new_latents, summed = reduce(outgoing, grad_latents, grads, frames)
    norm = 1.0 / math.sqrt(frames * total_rows * COLS)
    summed = summed.reshape(-1, width).astype(F32) * norm
    return (
        coded[None],
        new_latents[None],
        summed[:width],
        summed[width : 2 * width],
        summed[2 * width : 3 * width],
        summed[3 * width :].reshape(3, width, width),
    )


def solution(mesh):
    tok = P(("groups", "frame"), "row", None)
    frm = P(("groups", "frame"))
    placed = (tok, P(("groups", "frame"), None), frm, frm, P(), P(), P(), P(), P(), tok)
    return jax.shard_map(
        local,
        mesh=mesh,
        in_specs=placed,
        out_specs=(
            tok, tok, P("groups", None), P("groups", None), P("groups", None),
            P("groups", None, None),
        ),
        check_vma=False,
    )
```

```python
import functools
import math

import jax
import jax.numpy as jnp
from jax import lax
from jax.experimental import pallas as pl
from jax.experimental.pallas import tpu as pltpu
from jax.sharding import PartitionSpec as P

HEADS = 8
DH = 32
COLS = 64
QBLK = 4
WMAX = 2

SCORE_SCALE = 1.5 / math.sqrt(DH)
LOG2E = math.log2(math.e)
BF = jnp.bfloat16
F32 = jnp.float32


def mm(a, b, ca=1, cb=0):
    return lax.dot_general(a, b, (((ca,), (cb,)), ((), ())), preferred_element_type=F32)


def attention_kernel(
    meta_ref, buf_hbm, halo_hbm, x_hbm, q_hbm, qt_hbm, do_hbm, dot_hbm, resid_hbm,
    sp_ref, vp_ref, op_ref,
    residual_ref, hidden_ref, base_ref, part_ref, gs_ref, gv_ref, go_ref,
    xs_ref, k_ref, v_ref, kt_ref, vt_ref, mixt_ref, dqt_ref, dk_ref, dv_ref,
    s_scr, dp_scr, p_scr, ds_scr, qm_scr, dom_scr,
    x_ref, q_ref, qt_ref, do_ref, dot_ref, resid_ref, sems,
):
    tokens, width = q_ref.shape
    nq = QBLK * COLS
    span = (QBLK + 2 * WMAX) * COLS
    rows = span // COLS
    blocks = tokens // nq
    half = width // 2
    per_half = HEADS // 2
    lane = lax.broadcasted_iota(jnp.int32, (1, width), 1) // DH
    sub = lax.broadcasted_iota(jnp.int32, (half, 1), 0) // DH

    dk_ref[...] = jnp.zeros_like(dk_ref)
    dv_ref[...] = jnp.zeros_like(dv_ref)
    rim = WMAX * COLS
    window = meta_ref[2]
    row_id = meta_ref[3]
    first_row = row_id * (tokens // COLS)
    total_rows = meta_ref[4]
    bottom = rim + tokens
    held = pl.multiple_of(jnp.where(row_id == 0, bottom, 0), rim)
    empty = pl.multiple_of(jnp.where(row_id == 0, 0, bottom), rim)
    moves = []
    for s in range(2):
        kind = meta_ref[s]
        moves.append((buf_hbm.at[kind], xs_ref.at[s, pl.ds(rim, tokens)]))
        moves.append((halo_hbm.at[kind], xs_ref.at[s, pl.ds(held, rim)]))
    moves += [
        (q_hbm, q_ref), (do_hbm, do_ref), (qt_hbm, qt_ref), (dot_hbm, dot_ref),
        (x_hbm, x_ref), (resid_hbm, resid_ref),
    ]
    copies = [
        pltpu.make_async_copy(source, target, sems.at[i])
        for i, (source, target) in enumerate(moves)
    ]
    for move in copies:
        move.start()
    for s in range(2):
        xs_ref[s, pl.ds(empty, rim), :] = jnp.zeros((rim, width), BF)
        copies[2 * s].wait()
        copies[2 * s + 1].wait()
        xs = xs_ref[s]
        keys = mm(xs, sp_ref[...]).astype(BF)
        vals = mm(xs, vp_ref[...]).astype(BF)
        k_ref[s] = keys
        v_ref[s] = vals
        kt_ref[s] = keys.T
        vt_ref[s] = vals.T
    for move in copies[4:]:
        move.wait()
    query_row = lax.broadcasted_iota(jnp.int32, (1, nq), 1) // COLS

    def bias_row(b, c):
        key_row = first_row + b * QBLK + c - WMAX
        reach = jnp.where((key_row >= 0) & (key_row < total_rows), window, -1)
        return jnp.where(jnp.abs(c - WMAX - query_row) <= reach, 0.0, -jnp.inf).astype(F32)

    for b in range(blocks):
        q0 = b * nq
        qb = q_ref[q0 : q0 + nq, :]
        dob = do_ref[q0 : q0 + nq, :]
        for h in range(HEADS):
            keep = lane == h
            qm_scr[h * nq : (h + 1) * nq, :] = jnp.where(keep, qb, jnp.zeros_like(qb))
            dom_scr[h * nq : (h + 1) * nq, :] = jnp.where(keep, dob, jnp.zeros_like(dob))

        for hf in range(2):
            f0 = hf * half
            qth = qt_ref[f0 : f0 + half, q0 : q0 + nq]
            doth = dot_ref[f0 : f0 + half, q0 : q0 + nq]

            def one_head(hh, carry, hf=hf, f0=f0, qth=qth, doth=doth, q0=q0, b=b):
                keep = sub == hh
                qtm = jnp.where(keep, qth, jnp.zeros_like(qth))
                dotm = jnp.where(keep, doth, jnp.zeros_like(doth))
                for s in range(2):
                    s_scr[s * span : (s + 1) * span, :] = mm(
                        k_ref[s, q0 : q0 + span, f0 : f0 + half], qtm
                    )
                    dp_scr[s * span : (s + 1) * span, :] = mm(
                        v_ref[s, q0 : q0 + span, f0 : f0 + half], dotm
                    )
                m8 = jnp.full((8, nq), -jnp.inf, F32)
                for c in range(2 * rows):
                    x = s_scr[c * COLS : (c + 1) * COLS, :].reshape(COLS // 8, 8, nq)
                    m8 = jnp.maximum(m8, jnp.max(x, axis=0) + bias_row(b, c % rows))
                m = jnp.max(m8, axis=0, keepdims=True)
                kk = SCORE_SCALE * LOG2E
                l8 = jnp.zeros((8, nq), F32)
                u8 = jnp.zeros((8, nq), F32)
                for c in range(2 * rows):
                    sl = slice(c * COLS, (c + 1) * COLS)
                    off = (bias_row(b, c % rows) - m) * kk
                    p = jnp.exp2(s_scr[sl, :] * kk + off)
                    s_scr[sl, :] = p
                    l8 = l8 + jnp.sum(p.reshape(COLS // 8, 8, nq), axis=0)
                    u8 = u8 + jnp.sum((p * dp_scr[sl, :]).reshape(COLS // 8, 8, nq), axis=0)
                inv = 1.0 / jnp.sum(l8, axis=0, keepdims=True)
                ci = inv * SCORE_SCALE
                inner = jnp.sum(u8, axis=0, keepdims=True) * inv * ci
                col = pl.multiple_of((hf * per_half + hh) * nq, nq)
                for c in range(2 * rows):
                    sl = slice(c * COLS, (c + 1) * COLS)
                    p = s_scr[sl, :]
                    p_scr[sl, pl.ds(col, nq)] = (p * inv).astype(BF)
                    ds_scr[sl, pl.ds(col, nq)] = (p * (dp_scr[sl, :] * ci - inner)).astype(BF)
                r0 = pl.multiple_of(f0 + hh * DH, DH)
                mix = jnp.zeros((DH, nq), F32)
                dq = jnp.zeros((DH, nq), F32)
                for s in range(2):
                    ks = slice(s * span, (s + 1) * span)
                    mix = mix + mm(
                        vt_ref[s, pl.ds(r0, DH), q0 : q0 + span], p_scr[ks, pl.ds(col, nq)]
                    )
                    dq = dq + mm(
                        kt_ref[s, pl.ds(r0, DH), q0 : q0 + span], ds_scr[ks, pl.ds(col, nq)]
                    )
                mixt_ref[pl.ds(r0, DH), q0 : q0 + nq] = mix.astype(BF)
                dqt_ref[pl.ds(r0, DH), q0 : q0 + nq] = dq
                return carry

            lax.fori_loop(0, per_half, one_head, 0)

        for s in range(2):
            ks = slice(s * span, (s + 1) * span)
            dk_ref[s, q0 : q0 + span, :] += mm(ds_scr[ks, :], qm_scr[...])
            dv_ref[s, q0 : q0 + span, :] += mm(p_scr[ks, :], dom_scr[...])

    dq = dqt_ref[...].T.astype(BF)
    base_ref[...] = resid_ref[...] + mm(dq, sp_ref[...], 1, 1)
    mixt = mixt_ref[...]
    go_ref[...] = mm(mixt, resid_ref[...].astype(BF))
    residual = x_ref[...].astype(F32) + mm(mixt.T, op_ref[...])
    residual_ref[...] = residual
    hidden_ref[...] = residual.astype(BF)
    gs = mm(x_ref[...].T, dq)
    gv = jnp.zeros((width, width), F32)
    for s in range(2):
        dk = dk_ref[s].astype(BF)
        dv = dv_ref[s].astype(BF)
        part_ref[s] = mm(dk, sp_ref[...], 1, 1) + mm(dv, vp_ref[...], 1, 1)
        xst = xs_ref[s].T
        gs = gs + mm(xst, dk)
        gv = gv + mm(xst, dv)
    gs_ref[...] = gs
    gv_ref[...] = gv


def attention(meta, buf, halo, x, q, qt, do, dot, resid, shared, value, output):
    tokens, width = q.shape
    ext = tokens + 2 * WMAX * COLS
    nq = QBLK * COLS
    keys = 2 * (QBLK + 2 * WMAX) * COLS
    vm = pl.BlockSpec(memory_space=pltpu.VMEM)
    full = jax.ShapeDtypeStruct((tokens, width), F32)
    square = jax.ShapeDtypeStruct((width, width), F32)
    return pl.pallas_call(
        attention_kernel,
        out_shape=(
            full,
            jax.ShapeDtypeStruct((tokens, width), BF),
            full,
            jax.ShapeDtypeStruct((2, ext, width), F32),
            square, square, square,
        ),
        in_specs=[pl.BlockSpec(memory_space=pltpu.SMEM)]
        + [pl.BlockSpec(memory_space=pltpu.MemorySpace.HBM)] * 8
        + [vm] * 3,
        out_specs=(vm,) * 7,
        scratch_shapes=[
            pltpu.VMEM((2, ext, width), BF),
            pltpu.VMEM((2, ext, width), BF),
            pltpu.VMEM((2, ext, width), BF),
            pltpu.VMEM((2, width, ext), BF),
            pltpu.VMEM((2, width, ext), BF),
            pltpu.VMEM((width, tokens), BF),
            pltpu.VMEM((width, tokens), F32),
            pltpu.VMEM((2, ext, width), F32),
            pltpu.VMEM((2, ext, width), F32),
            pltpu.VMEM((keys, nq), F32),
            pltpu.VMEM((keys, nq), F32),
            pltpu.VMEM((keys, HEADS * nq), BF),
            pltpu.VMEM((keys, HEADS * nq), BF),
            pltpu.VMEM((HEADS * nq, width), BF),
            pltpu.VMEM((HEADS * nq, width), BF),
            pltpu.VMEM((tokens, width), BF),
            pltpu.VMEM((tokens, width), BF),
            pltpu.VMEM((width, tokens), BF),
            pltpu.VMEM((tokens, width), BF),
            pltpu.VMEM((width, tokens), BF),
            pltpu.VMEM((tokens, width), F32),
            pltpu.SemaphoreType.DMA((10,)),
        ],
        compiler_params=pltpu.CompilerParams(vmem_limit_bytes=66_000_000),
        cost_estimate=pl.CostEstimate(
            flops=int(2e10), bytes_accessed=int(8e6), transcendentals=int(4e6)
        ),
        name="attention",
    )(meta, buf, halo, x, q, qt, do, dot, resid, shared, value, output)


MESH = pl.DeviceIdType.MESH
CHUNKS = 4


def greet(targets):
    barrier = pltpu.get_barrier_semaphore()
    count = 0
    for exists, device in targets:

        @pl.when(exists)
        def _(device=device):
            pl.semaphore_signal(barrier, inc=1, device_id=device, device_id_type=MESH)

        count = count + jnp.where(exists, 1, 0)
    pl.semaphore_wait(barrier, count)


def fetch_kernel(
    frames, level_ref, x_ref, ct_ref, qs_ref, sp_ref, op_ref, taps_ref,
    buf_ref, halo_ref, q_ref, qt_ref, do_ref, dot_ref, gzb_ref, resid_ref, gain_ref,
    cth_ref, ext_ref, ssem, rsem, hs, hr, cs, cr,
):
    f = lax.axis_index("frame")
    r = lax.axis_index("row")
    tokens = x_ref.shape[0]
    odd = lax.rem(f, 2)
    pair = f + 1 - 2 * odd
    lo2, hi2, lo4, hi4 = f >= 2, f + 2 < frames, f >= 4, f + 4 < frames
    side = ((odd == 1) & (f + 1 < frames)) | ((odd == 0) & (f >= 1))
    always = f >= 0
    have = (lo2, hi2, always, lo4, hi4, side)
    partner = {"row": 1 - r}
    up, down, across = {"frame": f + 2}, {"frame": f - 2}, {"frame": pair}
    greet(((hi2, up), (lo2, down), (always, across), (always, partner)))

    edge = ct_ref.shape[0] - COLS
    ct_copy = pltpu.make_async_remote_copy(
        ct_ref.at[pl.ds(pl.multiple_of((1 - r) * edge, COLS), COLS)], cth_ref, cs, cr,
        device_id=partner, device_id_type=MESH,
    )
    ct_copy.start()
    step = tokens // CHUNKS

    def copy(kind, c, source, device):
        part = pl.ds(c * step, step)
        return pltpu.make_async_remote_copy(
            source.at[part], buf_ref.at[kind, part], ssem.at[kind, c], rsem.at[kind, c],
            device_id=device, device_id_type=MESH,
        )

    for c in range(CHUNKS):

        @pl.when(hi2)
        def _():
            copy(0, c, x_ref, up).start()

        @pl.when(lo2)
        def _():
            copy(1, c, x_ref, down).start()

        copy(2, c, x_ref, across).start()

    for c in range(CHUNKS):

        @pl.when(lo2)
        def _():
            copy(0, c, x_ref, across).wait_recv()

        @pl.when(lo2 & hi2)
        def _():
            copy(3, c, buf_ref.at[0], up).start()

        @pl.when(lo2 & (odd == 1))
        def _():
            copy(5, c, buf_ref.at[0], across).start()

        @pl.when(hi2)
        def _():
            copy(1, c, x_ref, across).wait_recv()

        @pl.when(hi2 & lo2)
        def _():
            copy(4, c, buf_ref.at[1], down).start()

        @pl.when(hi2 & (odd == 0))
        def _():
            copy(5, c, buf_ref.at[1], across).start()

    level = lax.broadcasted_iota(jnp.int32, (qs_ref.shape[0], 1), 0)
    gain = jnp.sum(
        jnp.where(level == level_ref[0], qs_ref[...], 0.0), axis=0, keepdims=True
    )
    gain_ref[...] = gain
    queries = mm(x_ref[...], sp_ref[...]).astype(BF)
    q_ref[...] = queries
    qt_ref[...] = queries.T
    grad_z = ct_ref[...].astype(F32) * gain
    grad_zb = grad_z.astype(BF)
    gzb_ref[...] = grad_zb
    ct_copy.wait()
    outer = (cth_ref[...].astype(F32) * gain).astype(BF)
    blank = jnp.zeros_like(outer)
    ext_ref[COLS : COLS + tokens, :] = grad_zb

    @pl.when(r == 0)
    def _():
        ext_ref[:COLS, :] = blank
        ext_ref[COLS + tokens :, :] = outer

    @pl.when(r != 0)
    def _():
        ext_ref[:COLS, :] = outer
        ext_ref[COLS + tokens :, :] = blank

    resid = grad_z
    for t in range(3):
        resid = resid + mm(ext_ref[(2 - t) * COLS : (2 - t) * COLS + tokens, :], taps_ref[t], 1, 1)
    resid_ref[...] = resid
    grad_mixed = mm(resid.astype(BF), op_ref[...], 1, 1).astype(BF)
    do_ref[...] = grad_mixed
    dot_ref[...] = grad_mixed.T

    rim = WMAX * COLS
    start = pl.multiple_of((1 - r) * (tokens - rim), rim)

    def halo(kind):
        return pltpu.make_async_remote_copy(
            buf_ref.at[kind, pl.ds(start, rim)], halo_ref.at[kind], hs.at[kind], hr.at[kind],
            device_id=partner, device_id_type=MESH,
        )

    for kind in range(6):

        @pl.when(have[kind])
        def _():
            if kind > 1:
                for c in range(CHUNKS):
                    copy(kind, c, x_ref, across).wait_recv()
            halo(kind).start()

    sent = (hi2, lo2, always, lo2 & hi2, lo2 & hi2, (lo2 & (odd == 1)) | (hi2 & (odd == 0)))
    for kind in range(6):

        @pl.when(have[kind])
        def _():
            halo(kind).wait()

        @pl.when(sent[kind])
        def _():
            for c in range(CHUNKS):
                copy(kind, c, x_ref, across).wait_send()


def fetch(level, tokens, cotangent, scale, shared, output, taps, frames):
    count, width = tokens.shape
    vm = pl.BlockSpec(memory_space=pltpu.VMEM)
    dma = pltpu.SemaphoreType.DMA
    rows = jax.ShapeDtypeStruct((count, width), BF)
    columns = jax.ShapeDtypeStruct((width, count), BF)
    return pl.pallas_call(
        functools.partial(fetch_kernel, frames),
        out_shape=(
            jax.ShapeDtypeStruct((6, count, width), BF),
            jax.ShapeDtypeStruct((6, WMAX * COLS, width), BF),
            rows, columns, rows, columns, rows,
            jax.ShapeDtypeStruct((count, width), F32),
            jax.ShapeDtypeStruct((1, width), F32),
        ),
        in_specs=[pl.BlockSpec(memory_space=pltpu.SMEM)] + [vm] * 6,
        out_specs=(vm,) * 9,
        scratch_shapes=[
            pltpu.VMEM((COLS, width), BF),
            pltpu.VMEM((count + 2 * COLS, width), BF),
            dma((6, CHUNKS)), dma((6, CHUNKS)), dma((6,)), dma((6,)), dma(()), dma(()),
        ],
        compiler_params=pltpu.CompilerParams(collective_id=0, has_side_effects=True),
        name="fetch",
    )(level, tokens, cotangent, scale, shared, output, taps)


def reduce_kernel(
    frames, out_ref, base_ref, w_ref, lat_ref, wsum_ref,
    rb, sb, wp, ws, xr, wr, ssem, rsem, ps, pr, xs, xg,
    rs_s, rs_r, ag_s, ag_r, px_s, px_r, fw_s, fw_r,
):
    f = lax.axis_index("frame")
    r = lax.axis_index("row")
    tokens = base_ref.shape[0]
    odd = lax.rem(f, 2)
    pair = f + 1 - 2 * odd
    lo2, hi2, lo4, hi4 = f >= 2, f + 2 < frames, f >= 4, f + 4 < frames
    always = f >= 0
    side = ((odd == 1) & (f + 1 < frames)) | ((odd == 0) & (f >= 1))
    relay = ((odd == 1) & lo2) | ((odd == 0) & hi2)
    partner = {"row": 1 - r}
    up, down, across = {"frame": f + 2}, {"frame": f - 2}, {"frame": pair}

    barrier = pltpu.get_barrier_semaphore()
    pl.semaphore_signal(barrier, inc=1, device_id=partner, device_id_type=MESH)
    pl.semaphore_signal(barrier, inc=1, device_id=across, device_id_type=MESH)
    deep = frames // 2
    place = f // 2
    mine = odd * deep
    theirs = deep - mine

    def hello(k, carry):
        pl.semaphore_signal(
            barrier, inc=1, device_id={"frame": 2 * lax.rem(place + k, deep) + odd},
            device_id_type=MESH,
        )
        return carry

    lax.fori_loop(1, deep, hello, 0)
    pl.semaphore_wait(barrier, deep + 1)

    step = tokens // CHUNKS
    sent = (hi2, lo2, always, hi4, lo4, side)
    got = (lo2, hi2, always, lo2 & hi2, lo2 & hi2, relay)
    device = (up, down, across, up, down, across)

    def copy(kind, c, source):
        part = pl.ds(c * step, step)
        return pltpu.make_async_remote_copy(
            source.at[part], rb.at[kind, part], ssem.at[kind, c], rsem.at[kind, c],
            device_id=device[kind], device_id_type=MESH,
        )

    halves = pltpu.make_async_remote_copy(
        w_ref.at[1 - r], wp, ps, pr, device_id=partner, device_id_type=MESH
    )
    halves.start()
    for c in range(CHUNKS):
        for kind in (3, 4, 5):

            @pl.when(sent[kind])
            def _():
                copy(kind, c, out_ref.at[kind]).start()

    for kind in (0, 1, 3, 4, 5):

        @pl.when(jnp.logical_not(got[kind]))
        def _():
            rb[kind, :, :] = jnp.zeros((tokens, rb.shape[2]), BF)

    halves.wait()
    other_side = pl.ds(theirs, deep)
    own_side = pl.ds(mine, deep)
    ws[other_side] = (w_ref[r, other_side] + wp[other_side]).astype(BF)
    swap = pltpu.make_async_remote_copy(
        ws.at[other_side], xr, xs, xg, device_id=across, device_id_type=MESH
    )
    swap.start()

    def column(index, source, target, s_sem, r_sem, k, slot):
        return pltpu.make_async_remote_copy(
            source, target, s_sem.at[k], r_sem.at[slot],
            device_id={"frame": 2 * index + odd}, device_id_type=MESH,
        )

    def scatter(k):
        index = lax.rem(place + k, deep)
        return column(index, ws.at[mine + index], wr.at[place], rs_s, rs_r, k, place)

    def arrived(k):
        index = lax.rem(place - k + deep, deep)
        return index, column(index, ws.at[mine + index], wr.at[index], rs_s, rs_r, k, index)

    def gather(k):
        index = lax.rem(place + k, deep)
        block = wsum_ref.at[r, mine + place]
        return column(index, block, block, ag_s, ag_r, k, place)

    def gathered(k):
        index = lax.rem(place - k + deep, deep)
        block = wsum_ref.at[r, mine + index]
        return index, column(index, block, block, ag_s, ag_r, k, index)

    def cross(side, index):
        block = wsum_ref.at[r, side + index]
        return pltpu.make_async_remote_copy(
            block, block, px_s.at[index], px_r.at[index],
            device_id=across, device_id_type=MESH,
        )

    def forward(j, own):
        return pltpu.make_async_remote_copy(
            wsum_ref.at[own, j], wsum_ref.at[own, j], fw_s.at[j], fw_r.at[j],
            device_id=partner, device_id_type=MESH,
        )

    def run(body):
        lax.fori_loop(1, deep, lambda k, carry: (body(k), carry)[1], 0)

    for c in range(CHUNKS):
        copy(2, c, out_ref.at[2]).start()
    swap.wait()
    ws[own_side] = (w_ref[r, own_side] + wp[own_side] + xr[...].astype(F32)).astype(BF)
    run(lambda k: scatter(k).start())

    even = jnp.where(odd == 0, 1.0, 0.0).astype(F32)
    for c in range(CHUNKS):
        part = slice(c * step, (c + 1) * step)
        for kind in (3, 4, 5):

            @pl.when(got[kind])
            def _():
                copy(kind, c, out_ref.at[kind]).wait_recv()

        extra = rb[5, part, :].astype(F32)
        rising = out_ref[0, part, :].astype(F32) + rb[3, part, :].astype(F32) + extra * even
        falling = (
            out_ref[1, part, :].astype(F32) + rb[4, part, :].astype(F32) + extra * (1.0 - even)
        )
        sb[0, part, :] = rising.astype(BF)
        sb[1, part, :] = falling.astype(BF)

        @pl.when(hi2)
        def _():
            copy(0, c, sb.at[0]).start()

        @pl.when(lo2)
        def _():
            copy(1, c, sb.at[1]).start()

    def add_piece(k, total):
        source, waiting = arrived(k)
        waiting.wait_recv()
        return total + wr[source].astype(F32)

    here = mine + place
    total = lax.fori_loop(
        1, deep, add_piece, w_ref[r, here] + wp[here] + xr[place].astype(F32)
    )
    wsum_ref[r, here] = total.astype(BF)
    run(lambda k: gather(k).start())
    cross(mine, place).start()
    forward(here, r).start()

    for c in range(CHUNKS):
        part = slice(c * step, (c + 1) * step)
        for kind in (0, 1, 2):

            @pl.when(got[kind])
            def _():
                copy(kind, c, out_ref.at[kind]).wait_recv()

        lat_ref[part, :] = (
            base_ref[part, :]
            + rb[0, part, :].astype(F32)
            + rb[1, part, :].astype(F32)
            + rb[2, part, :].astype(F32)
        ).astype(BF)

    def pass_on(k):
        index, waiting = gathered(k)
        waiting.wait_recv()
        cross(mine, index).start()
        forward(mine + index, r).start()

    run(pass_on)

    def crossed(index, carry):
        cross(theirs, index).wait_recv()
        forward(theirs + index, r).start()
        return carry

    lax.fori_loop(0, deep, crossed, 0)

    def finish(k):
        scatter(k).wait_send()
        gather(k).wait_send()

    run(finish)

    def done(index, carry):
        cross(mine, index).wait_send()
        return carry

    lax.fori_loop(0, deep, done, 0)

    def last(j, carry):
        forward(j, r).wait_send()
        forward(j, 1 - r).wait_recv()
        return carry

    lax.fori_loop(0, frames, last, 0)
    for kind in range(6):

        @pl.when(sent[kind])
        def _():
            for c in range(CHUNKS):
                copy(kind, c, out_ref.at[kind]).wait_send()


def reduce(outgoing, base, grads, frames):
    count, width = base.shape
    vm = pl.BlockSpec(memory_space=pltpu.VMEM)
    dma = pltpu.SemaphoreType.DMA
    pieces = grads.shape[1:]
    return pl.pallas_call(
        functools.partial(reduce_kernel, frames),
        out_shape=(
            jax.ShapeDtypeStruct((count, width), BF),
            jax.ShapeDtypeStruct(grads.shape, BF),
        ),
        in_specs=[vm] * 3,
        out_specs=(vm,) * 2,
        scratch_shapes=[
            pltpu.VMEM((6, count, width), BF),
            pltpu.VMEM((2, count, width), BF),
            pltpu.VMEM(pieces, F32),
            pltpu.VMEM(pieces, BF),
            pltpu.VMEM((frames // 2,) + pieces[1:], BF),
            pltpu.VMEM((frames // 2,) + pieces[1:], BF),
            dma((6, CHUNKS)), dma((6, CHUNKS)), dma(()), dma(()), dma(()), dma(()),
            dma((frames // 2,)), dma((frames // 2,)), dma((frames // 2,)), dma((frames // 2,)),
            dma((frames // 2,)), dma((frames // 2,)), dma((frames,)), dma((frames,)),
        ],
        compiler_params=pltpu.CompilerParams(collective_id=1, has_side_effects=True),
        name="reduce",
    )(outgoing, base, grads)


def from_partner(value):
    return lax.ppermute(value, "row", [(0, 1), (1, 0)])


def row_halo(array, row_id, width):
    length = array.shape[-3]
    first = lax.slice_in_dim(array, 0, width, axis=array.ndim - 3)
    last = lax.slice_in_dim(array, length - width, length, axis=array.ndim - 3)
    got = from_partner(jnp.where(row_id == 0, last, first))
    zero = jnp.zeros_like(got)
    before = jnp.where(row_id == 0, zero, got)
    after = jnp.where(row_id == 0, got, zero)
    return jnp.concatenate([before, array, after], axis=array.ndim - 3)


def local(
    latents, ref_frames, windows, quant_level, quant_scale,
    shared_proj, value_proj, output_proj, conv_taps, cotangent,
):
    width = latents.shape[2]
    rows_dev = latents.shape[1] // COLS
    row_devs = lax.axis_size("row")
    total_rows = rows_dev * row_devs
    frame_id = lax.axis_index("frame")
    row_id = lax.axis_index("row")
    own_refs = ref_frames[0]
    ext_rows = rows_dev + 2 * WMAX
    grid = (rows_dev, COLS, width)
    tokens = latents[0]
    frames = lax.axis_size("frame")
    odd = frame_id % 2
    sources = (
        frame_id - 2, frame_id + 2, frame_id + 1 - 2 * odd,
        frame_id - 4, frame_id + 4, frame_id - 1 + 2 * odd,
    )
    buf, halo, q, qt, do, dot, grad_zb, grad_resid, gain = fetch(
        quant_level, tokens, cotangent[0], quant_scale, shared_proj, output_proj, conv_taps, frames
    )
    kinds = jnp.zeros((2,), jnp.int32)
    for kind, source in enumerate(sources):
        kinds = jnp.where(own_refs == source, kind, kinds)
    rest = jnp.stack([windows[0], row_id, jnp.int32(total_rows)]).astype(jnp.int32)
    meta = jnp.concatenate([kinds, rest])
    residual, hidden, grad_latents, partial, grad_shared, grad_values, grad_output = attention(
        meta, buf, halo, tokens, q, qt, do, dot, grad_resid, shared_proj, value_proj, output_proj
    )
    hidden_ext = row_halo(hidden.reshape(grid), row_id, 1).reshape(-1, width)
    context = residual
    for t in range(3):
        context = context + mm(hidden_ext[t * COLS : (t + rows_dev) * COLS], conv_taps[t])
    coded = (context * gain).astype(BF)

    partial = partial.reshape(2, ext_rows, COLS, width)
    upper = partial[:, :WMAX]
    lower = partial[:, WMAX + rows_dev :]
    got = from_partner(jnp.where(row_id == 0, lower, upper).astype(BF)).astype(F32)
    filler = jnp.zeros((2, rows_dev - WMAX, COLS, width), F32)
    middle = (
        partial[:, WMAX : WMAX + rows_dev]
        + jnp.concatenate([jnp.where(row_id == 0, 0.0, got), filler], axis=1)
        + jnp.concatenate([filler, jnp.where(row_id == 0, got, 0.0)], axis=1)
    )
    targets = (
        frame_id + 2, frame_id - 2, frame_id + 1 - 2 * odd,
        frame_id + 4, frame_id - 4, frame_id - 1 + 2 * odd,
    )
    outgoing = jnp.stack(
        [
            jnp.sum(jnp.where((own_refs == t).reshape(2, 1, 1, 1), middle, 0.0), axis=0)
            .astype(BF)
            .reshape(-1, width)
            for t in targets
        ]
    )
    grad_taps = jnp.stack(
        [mm(hidden_ext[t * COLS : (t + rows_dev) * COLS], grad_zb, 0, 0) for t in range(3)]
    )
    stacked = jnp.concatenate(
        [grad_shared, grad_values, grad_output, grad_taps.reshape(-1, width)], axis=0
    )
    grads = stacked.reshape(2, frames, stacked.shape[0] // (2 * frames), width)
    new_latents, summed = reduce(outgoing, grad_latents, grads, frames)
    norm = 1.0 / math.sqrt(frames * total_rows * COLS)
    summed = summed.reshape(-1, width).astype(F32) * norm
    return (
        coded[None],
        new_latents[None],
        summed[:width],
        summed[width : 2 * width],
        summed[2 * width : 3 * width],
        summed[3 * width :].reshape(3, width, width),
    )


def solution(mesh):
    tok = P(("groups", "frame"), "row", None)
    frm = P(("groups", "frame"))
    placed = (tok, P(("groups", "frame"), None), frm, frm, P(), P(), P(), P(), P(), tok)
    return jax.shard_map(
        local,
        mesh=mesh,
        in_specs=placed,
        out_specs=(
            tok, tok, P("groups", None), P("groups", None), P("groups", None),
            P("groups", None, None),
        ),
        check_vma=False,
    )
```
